32 devices in a mesh: region: 4 (over z), row: 2 (over core), col: 4 (over y, x).
Axes of the slice: x: 2, y: 2, z: 4, core: 2. Of those that a mesh axis runs over, the one named last changes fastest.
Arguments:
- cam_jac: bfloat16 [3, 2, 256, 16384], P(None, None, None, 'region'), may hold values from -1 to 1
- point_rows: bfloat16 [3, 2, 4, 16384], P(None, None, None, 'region'), may hold values from -6 to 6
- track_images: int32 [3, 16384], P(None, 'region'), may hold values from 0 to 3, as said below
- track_counts: int32 [4], replicated, may hold values from 1 to 4096, 8192 in all
Outputs:
- factor: float32 [1024, 1024], P(('region', 'row'), 'col')
- solved: float32 [1024], replicated
The draws below stay inside these ranges and needn't reach their ends.
Inputs may be any that keep to these rules, and one draw needn't show every extreme that they name: `track_images`: each track's 3 entries are different images of the slab. `track_counts`: entry r counts region r's live tracks, which fill its first slots; later slots hold data that no output reads. The counts sum to 8192, and one region has exactly 4096.
All inputs are finite; a program needn't handle non-finite values.
Results may differ from the reference program's by a relative error of at most 0.0036.
Values may be sent and summed in bfloat16 or wider, within the bound.
A program may use at most 128 MiB of HBM per device.

```python
import math
import jax
import jax.numpy as jnp
import numpy as np
from jax import lax

PARAMS = 256
SLAB_IMAGES = 4
VIEWS = 3
BLOCK = 256
MEAN_TRACKS = 2048
SLOTS = 4096
REGIONS = 4
TRACKS = 16384
SLAB = 1024


def draw_track_images(key, part):
    first = jax.random.randint(key, (TRACKS,), 0, SLAB_IMAGES)
    offsets = jnp.arange(VIEWS, dtype=jnp.int32)[:, None]
    return ((first[None, :] + offsets) % SLAB_IMAGES).astype(jnp.int32)


def draw_cam_jac(key, part):
    subkeys = jax.random.split(key, 3)
    common = jnp.clip(jax.random.normal(subkeys[0], (1, 2, 1, TRACKS), jnp.float32), -4.0, 4.0)
    shared = jnp.clip(jax.random.normal(subkeys[1], (1, 2, PARAMS, TRACKS), jnp.float32), -4.0, 4.0)
    single = jnp.clip(jax.random.normal(subkeys[2], (VIEWS, 2, PARAMS, TRACKS), jnp.float32), -4.0, 4.0)
    entries = 0.7 * common + 2.0 * shared + single
    normalizer = 1.0 / jnp.sqrt(jnp.float32(5.0 * MEAN_TRACKS * REGIONS))
    return (entries * normalizer).astype(jnp.bfloat16)


def draw_point_rows(key, part):
    subkeys = jax.random.split(key, 3)
    ground = jax.random.normal(subkeys[0], (1, 2, 3, TRACKS), jnp.float32)
    single = jax.random.normal(subkeys[1], (VIEWS, 2, 3, TRACKS), jnp.float32)
    errors = jax.random.normal(subkeys[2], (VIEWS, 2, 1, TRACKS), jnp.float32)
    coords = ground + 0.3 * single
    joined = jnp.concatenate([coords, errors], axis=2)
    return jnp.clip(joined, -6.0, 6.0).astype(jnp.bfloat16)


def split_up(number_of, total, limit, lean):
    portions = [(1 << 20) // math.isqrt(grade ** lean) + 1 for grade in range(2, number_of + 1)]
    rest, given = total - limit - (number_of - 1), [1] * (number_of - 1)
    while rest > 0:
        movable = [i for i in range(number_of - 1) if given[i] < limit]
        pool, left = sum([portions[i] for i in movable]), rest
        for i in movable:
            extra = min(limit - given[i], max(1, left * portions[i] // pool), rest)
            given[i] = given[i] + extra
            rest = rest - extra
    return np.array([limit] + given)


def uneven(rng, number_of, total, reach, lean):
    if number_of == 2:
        one = jax.random.randint(rng, (), max(1, total - reach), min(reach, total - 1) + 1)
        return jnp.stack([one, total - one])
    tallies = jnp.asarray(split_up(number_of, total, reach, lean), jnp.int32)
    couples = (number_of - 1) // 2
    source_of, sink = tallies[1:1 + 2 * couples:2], tallies[2:2 + 2 * couples:2]
    room = jnp.minimum(source_of - 1, reach - sink)
    shifted = jax.random.randint(jax.random.fold_in(rng, 1), (couples,), 0, 1 << 20) % (room + 1)
    tallies = tallies.at[1:1 + 2 * couples:2].set(source_of - shifted).at[2:2 + 2 * couples:2].set(sink + shifted)
    return tallies[jax.random.permutation(jax.random.fold_in(rng, 2), number_of)]


def setup_inputs(seed: int = 0) -> dict:
    arg_keys = jax.random.split(jax.random.key(seed), 5)
    return {
        "cam_jac": draw_cam_jac(jax.random.fold_in(arg_keys[4], 71), 0),
        "point_rows": draw_point_rows(jax.random.fold_in(arg_keys[4], 71), 0),
        "track_images": draw_track_images(jax.random.fold_in(arg_keys[4], 71), 0),
        "track_counts": uneven(arg_keys[3], REGIONS, MEAN_TRACKS * REGIONS, SLOTS, 2).astype(jnp.int32),
    }


damping = 0.1
point_damping = 0.5

def lower_solve(factor_parts, first, second, third):
    diag_one, below_one, diag_two, below_far, below_two, diag_three = factor_parts
    out_one = first / diag_one
    out_two = (second - below_one * out_one) / diag_two
    out_three = (third - below_far * out_one - below_two * out_two) / diag_three
    return (out_one, out_two, out_three)

def block_terms(cam, points, selector):
    jac_point = points[:, :, 0:3].astype(jnp.float32)
    errors = points[:, :, 3].astype(jnp.float32)

    def entry(left, right):
        return lax.optimization_barrier(jnp.sum(jac_point[:, :, left] * jac_point[:, :, right], axis=(0, 1)))
    diag_one = jnp.sqrt(entry(0, 0) + point_damping)
    below_one = entry(1, 0) / diag_one
    below_far = entry(2, 0) / diag_one
    diag_two = jnp.sqrt(entry(1, 1) + point_damping - below_one * below_one)
    below_two = (entry(2, 1) - below_far * below_one) / diag_two
    diag_three = jnp.sqrt(entry(2, 2) + point_damping - below_far * below_far - below_two * below_two)
    factor_parts = (diag_one, below_one, diag_two, below_far, below_two, diag_three)
    coef = jnp.stack(lower_solve(factor_parts, jac_point[:, :, 0], jac_point[:, :, 1], jac_point[:, :, 2]), axis=0).astype(jnp.bfloat16)
    grads = [lax.optimization_barrier(jnp.sum(jac_point[:, :, comp] * errors, axis=(0, 1))) for comp in range(3)]
    point_step = jnp.stack(lower_solve(factor_parts, grads[0], grads[1], grads[2]), axis=0).astype(jnp.bfloat16)
    coef_wide = coef.astype(jnp.float32)
    products = cam[:, 0, :, None, :].astype(jnp.float32) * coef_wide[:, :, 0, :].transpose(1, 0, 2)[:, None, :, :]
    products = products + cam[:, 1, :, None, :].astype(jnp.float32) * coef_wide[:, :, 1, :].transpose(1, 0, 2)[:, None, :, :]
    schur = selector[0][:, None, None, :] * products[0][None]
    for view in range(1, selector.shape[0]):
        schur = schur + selector[view][:, None, None, :] * products[view][None]
    schur = schur.astype(jnp.bfloat16)
    pick = selector.astype(jnp.bfloat16)
    diagonal = jnp.einsum('krpb,kab->aprb', cam.astype(jnp.float32), pick.astype(jnp.float32), preferred_element_type=jnp.float32).astype(jnp.bfloat16)
    err_pick = (errors[None, :, :, :] * selector.transpose(1, 0, 2)[:, :, None, :]).astype(jnp.bfloat16)
    direct = jnp.einsum('krpb,akrb->ap', cam.astype(jnp.float32), err_pick.astype(jnp.float32), preferred_element_type=jnp.float32)
    coupled = jnp.einsum('apmb,mb->ap', schur.astype(jnp.float32), point_step.astype(jnp.float32), precision=lax.Precision.HIGHEST)
    return (schur, diagonal, direct - coupled)

def panel_factor(column, first_row, end_row):
    chol_block = jnp.linalg.cholesky(column[first_row:end_row])
    parts = [jnp.zeros((first_row, column.shape[1]), column.dtype), chol_block]
    if end_row < column.shape[0]:
        parts.append(lax.linalg.triangular_solve(chol_block, column[end_row:], left_side=False, lower=True, transpose_a=True))
    return jnp.concatenate(parts, axis=0)

def reference(cam_jac, point_rows, track_images, track_counts):

    def region_step(region, carry):
        count = track_counts[region]

        def block_step(block, inner):
            matrix, gradient = inner
            start = (region.astype(jnp.int32) * SLOTS + block.astype(jnp.int32) * BLOCK).astype(jnp.int32)
            cam = lax.dynamic_slice_in_dim(cam_jac, start, BLOCK, 3)
            points = lax.dynamic_slice_in_dim(point_rows, start, BLOCK, 3)
            images = lax.dynamic_slice_in_dim(track_images, start, BLOCK, 1)
            slot_ids = block.astype(jnp.int32) * BLOCK + jnp.arange(BLOCK, dtype=jnp.int32)
            live = (slot_ids < count).astype(jnp.float32)
            selector = (images[:, None, :] == jnp.arange(SLAB_IMAGES, dtype=jnp.int32)[None, :, None]).astype(jnp.float32) * live[None, None, :]
            schur, diagonal, grad = block_terms(cam, points, selector)
            flat = schur.reshape(SLAB, 3 * BLOCK)
            matrix = matrix - jnp.dot(flat.astype(jnp.float32), flat.T.astype(jnp.float32), preferred_element_type=jnp.float32)
            for image in range(SLAB_IMAGES):
                part = diagonal[image].reshape(PARAMS, 2 * BLOCK)
                update = jnp.dot(part.astype(jnp.float32), part.T.astype(jnp.float32), preferred_element_type=jnp.float32)
                matrix = matrix.at[image * PARAMS:(image + 1) * PARAMS, image * PARAMS:(image + 1) * PARAMS].add(update)
            gradient = gradient + grad.reshape(SLAB)
            return (matrix, gradient)
        blocks = ((count + BLOCK - 1) // BLOCK).astype(jnp.int32)
        return lax.fori_loop(jnp.int32(0), blocks, block_step, carry)
    start_state = (jnp.zeros((SLAB, SLAB), jnp.float32), jnp.zeros((SLAB,), jnp.float32))
    matrix, gradient = lax.fori_loop(0, REGIONS, region_step, start_state)
    matrix = matrix + damping * jnp.eye(SLAB, dtype=jnp.float32)
    columns = []
    pieces = []
    for panel in range(SLAB_IMAGES):
        first_row = panel * PARAMS
        end_row = first_row + PARAMS
        factored = panel_factor(matrix[:, first_row:end_row], first_row, end_row)
        columns.append(factored)
        part_z = lax.linalg.triangular_solve(factored[first_row:end_row], gradient[first_row:end_row][:, None], left_side=True, lower=True)[:, 0]
        pieces.append(part_z)
        below = jnp.concatenate([jnp.zeros((end_row, PARAMS), factored.dtype), factored[end_row:]], axis=0)
        gradient = gradient - jnp.dot(below, part_z, precision=lax.Precision.HIGHEST)
        matrix = matrix - jnp.dot(factored, factored.T, precision=lax.Precision.HIGHEST)
    return (jnp.concatenate(columns, axis=1), jnp.concatenate(pieces))
```

```python
import functools

import jax
import jax.numpy as jnp
from jax import lax
from jax.experimental import pallas as pl
from jax.experimental.pallas import tpu as pltpu
from jax.sharding import PartitionSpec as P

IMAGES = 4
CHUNKS = 4
ROWS = 8
BLOCK = 512
TILE = 128
GROUP = 16
EXTRA = 16
VMEM_LIMIT = 60 * 1024 * 1024

damping = 0.1
point_damping = 0.5

NT = (((1,), (1,)), ((), ()))
MESH = pl.DeviceIdType.MESH


def point_terms(pts):
    views = len(pts)
    pairs = [(k, r) for k in range(views) for r in range(2)]

    def entry(left, right):
        return sum(pts[k][r][left] * pts[k][r][right] for k, r in pairs)

    d1 = jnp.sqrt(entry(0, 0) + point_damping)
    b1 = entry(1, 0) / d1
    bf = entry(2, 0) / d1
    d2 = jnp.sqrt(entry(1, 1) + point_damping - b1 * b1)
    b2 = (entry(2, 1) - bf * b1) / d2
    d3 = jnp.sqrt(entry(2, 2) + point_damping - bf * bf - b2 * b2)

    def solve(first, second, third):
        o1 = first / d1
        o2 = (second - b1 * o1) / d2
        o3 = (third - bf * o1 - b2 * o2) / d3
        return [o.astype(jnp.bfloat16).astype(jnp.float32) for o in (o1, o2, o3)]

    coef = {(k, r): solve(*pts[k][r][0:3]) for k, r in pairs}
    step = solve(*[entry(c, 3) for c in range(3)])
    return coef, step


def units(params):
    half=params//2
    out=[(0,0,half),(0,half,half)]
    return out+[(b,0,params) for b in range(1,IMAGES)]


def unit_shapes(params):
    return [(2,CHUNKS,(IMAGES-b)*ROWS,w) for b,c0,w in units(params)]


def accumulate_kernel(block, pos_ref, cam_ref, pts_ref, img_ref, *refs):
    params=cam_ref.shape[2]
    us=units(params)
    outs=refs[:len(us)]; refs=refs[len(us):]
    accs=refs[:IMAGES]; rhs=refs[IMAGES:2*IMAGES]; lhs=refs[2*IMAGES:3*IMAGES]
    views=cam_ref.shape[0]
    own=params//4
    step=pl.program_id(0)
    count=pos_ref[lax.axis_index("region")]
    row_at=lax.axis_index("row"); col_at=lax.axis_index("col")
    start=(2*step+row_at)*block
    sub=16
    @pl.when(step==0)
    def _():
        for a in accs: a[...]=jnp.zeros_like(a)
    @pl.when(start<count)
    def _():
        slot=start+lax.broadcasted_iota(jnp.int32,(1,block),1)
        live=slot<count
        pts=[]
        for k in range(views):
            pts.append([])
            for r in range(2):
                wide=pts_ref[k,r].astype(jnp.float32)
                pts[k].append([wide[c:c+1,:] for c in range(4)])
        coef,y=point_terms(pts)
        images=[img_ref[k:k+1,:] for k in range(views)]
        zero=jnp.zeros((sub-2,block),jnp.float32)
        def pick(masks,values):
            out=jnp.zeros_like(values[0])
            for mask,value in zip(masks,values): out=jnp.where(mask,value,out)
            return out
        def widen(mask):
            return jnp.broadcast_to(mask.astype(jnp.float32),(sub,block)).astype(jnp.bfloat16)>0
        masks=[[(images[k]==a)&live for k in range(views)] for a in range(IMAGES)]
        wide=[[widen(m) for m in masks[a][:2]] for a in range(IMAGES)]
        c=[[[pick(masks[a],[coef[k,r][m] for k in range(views)]) for m in range(3)] for r in range(2)] for a in range(IMAGES)]
        held=[(masks[a][0]|masks[a][1]|masks[a][2]).astype(jnp.float32) for a in range(IMAGES)]
        err=[[pick(masks[a],[pts[k][r][3] for k in range(views)]) for r in range(2)] for a in range(IMAGES)]
        def chosen(a,at,r):
            j=[cam_ref[k,r,pl.ds(at,sub),:] for k in range(views)]
            return jnp.where(wide[a][0],j[0],jnp.where(wide[a][1],j[1],j[2]))
        mine=pl.multiple_of(col_at*own,own)
        for b in range(IMAGES):
            for i in range(params//sub):
                for r in range(2):
                    rhs[b][i*sub:(i+1)*sub,r*block:(r+1)*block]=chosen(b,i*sub,r)
            for a in range(b,IMAGES):
                x={}
                for r in range(2):
                    for s in range(2):
                        if a==b and s<r: x[r,s]=x[s,r]; continue
                        v=-(c[a][r][0]*c[b][s][0]+c[a][r][1]*c[b][s][1]+c[a][r][2]*c[b][s][2])
                        x[r,s]=v+held[a] if a==b and r==s else v
                for i in range(own//sub):
                    jac=[chosen(a,mine+i*sub,r).astype(jnp.float32) for r in range(2)]
                    for s in range(2):
                        v=jac[0]*x[0,s]+jac[1]*x[1,s]
                        lhs[b][(a-b)*own+i*sub:(a-b)*own+(i+1)*sub,s*block:(s+1)*block]=v.astype(jnp.bfloat16)
            depth=(IMAGES-b)*own
            for r in range(2):
                g=err[b][r]-(c[b][r][0]*y[0]+c[b][r][1]*y[1]+c[b][r][2]*y[2])
                near=g.astype(jnp.bfloat16).astype(jnp.float32)
                lhs[b][depth:depth+sub,r*block:(r+1)*block]=jnp.concatenate([near,g-near,zero],axis=0).astype(jnp.bfloat16)
            accs[b][...]+=lax.dot_general(lhs[b][...],rhs[b][...],NT,preferred_element_type=jnp.float32)
    @pl.when(step==pl.num_programs(0)-1)
    def _():
        half=params//2
        for b in range(IMAGES):
            acc=accs[b]
            depth=(IMAGES-b)*own
            sub8=lax.broadcasted_iota(jnp.int32,(8,half),0)
            grad=acc[depth:depth+1,:]+acc[depth+1:depth+2,:]
            one=jnp.broadcast_to(grad[:,0:half],(8,half))
            two=jnp.broadcast_to(grad[:,half:params],(8,half))
            held=acc[0:8,half:params]
            grad=jnp.where(sub8==0,one,jnp.where(sub8==1,two,held))
            acc[0:8,half:params]=jnp.where(col_at==0,grad,held)
        for out,(b,c0,w) in zip(outs,us):
            for core in range(2):
                for q in range(CHUNKS):
                    for a in range(IMAGES-b):
                        src=a*own+(core*CHUNKS+q)*ROWS
                        out[core,q,a*ROWS:(a+1)*ROWS,:]=accs[b][src:src+ROWS,c0:c0+w]
def accumulate(cam_jac,point_rows,track_images,pos,block=BLOCK):
    views,_,params,slots=cam_jac.shape
    own=params//4
    block=min(block,slots//2)
    def at(i,p):
        return jnp.minimum(2*i+lax.axis_index("row"),(p[lax.axis_index("region")]-1)//block)
    shapes=unit_shapes(params)
    return pl.pallas_call(
        functools.partial(accumulate_kernel, block),
        out_shape=[jax.ShapeDtypeStruct(s,jnp.float32) for s in shapes],
        grid_spec=pltpu.PrefetchScalarGridSpec(
            num_scalar_prefetch=1, grid=(slots//block//2,),
            in_specs=[pl.BlockSpec((views,2,params,block),lambda i,p:(0,0,0,at(i,p))),
                      pl.BlockSpec((views,2,4,block),lambda i,p:(0,0,0,at(i,p))),
                      pl.BlockSpec((views,block),lambda i,p:(0,at(i,p)))],
            out_specs=[pl.BlockSpec(s,lambda i,p:(0,0,0,0)) for s in shapes],
            scratch_shapes=[pltpu.VMEM(((IMAGES-b)*own+16,params),jnp.float32) for b in range(IMAGES)]+[
                pltpu.VMEM((params,2*block),jnp.bfloat16) for b in range(IMAGES)]+[
                pltpu.VMEM(((IMAGES-b)*own+16,2*block),jnp.bfloat16) for b in range(IMAGES)]),
        compiler_params=pltpu.CompilerParams(dimension_semantics=("arbitrary",),vmem_limit_bytes=VMEM_LIMIT),
        name="accumulate")(pos,cam_jac,point_rows,track_images)


def exchange_kernel(regions, params, *refs):
    count = len(units(params))
    parts, refs = refs[:count], refs[count:]
    alls, refs = refs[:count], refs[count:]
    recv1, refs = refs[:count], refs[count:]
    mine, refs = refs[:count], refs[count:]
    recv2, refs = refs[:count], refs[count:]
    s1, r1, s2, r2, s3, r3, s4, r4, s5, r5 = refs
    stride = regions // CHUNKS
    region_at = lax.axis_index("region")
    row_at = lax.axis_index("row")
    col_at = lax.axis_index("col")
    chunk_at = region_at // stride
    owner = lax.rem(region_at, stride) == 0

    def device(region, row, col):
        return {"region": region, "row": row, "col": col}

    def remote(src, dst, send, recv, to):
        return pltpu.make_async_remote_copy(
            src_ref=src, dst_ref=dst, send_sem=send, recv_sem=recv, device_id=to, device_id_type=MESH
        )

    def guarded(when, action):
        if when is True:
            action()
        else:
            pl.when(when)(action)

    owns = True if stride == 1 else owner
    partner = device(region_at, 1 - row_at, col_at)
    along = [device(lax.rem(region_at + d, regions), row_at, col_at) for d in range(1, regions)]
    cols = [lax.rem(col_at + d, IMAGES) for d in range(1, IMAGES)]
    across = [device(region_at, row_at, c) for c in cols]
    barrier = pltpu.get_barrier_semaphore()
    for peer in [partner] + along + across:
        pl.semaphore_signal(barrier, inc=1, device_id=peer, device_id_type=MESH)
    pl.semaphore_wait(barrier, regions + IMAGES - 1)
    sent = []

    def send(when, copy):
        sent.append((when, copy))
        guarded(when, lambda: copy.start())

    def swap_cores(u):
        return remote(parts[u].at[1 - row_at], recv1[u], s1.at[u], r1.at[u], partner)

    for u in range(count):
        send(True, swap_cores(u))

    def to_owner(u, d):
        chunk = lax.rem(chunk_at + d, CHUNKS)
        to = chunk * stride
        gap = lax.rem(to - region_at + regions, regions)
        return remote(
            mine[u].at[chunk], recv2[u].at[gap - 1], s2.at[u, d], r2.at[u, gap - 1], device(to, row_at, col_at)
        )

    def reduce_cores(u):
        swap_cores(u).wait_recv()
        mine[u][...] = parts[u][row_at] + recv1[u][...]
        for d in range(1, CHUNKS):
            send(True, to_owner(u, d))
        if stride > 1:
            send(jnp.logical_not(owner), to_owner(u, 0))

    def block(u, col, row):
        return alls[u].at[col, row]

    def reduce_regions(u):
        def total():
            value = mine[u][chunk_at]
            for gap in range(1, regions):
                remote(recv2[u].at[gap - 1], recv2[u].at[gap - 1], s2.at[u, 0], r2.at[u, gap - 1], partner).wait_recv()
                value = value + recv2[u][gap - 1]
            alls[u][col_at, row_at, chunk_at] = value

        guarded(owns, total)
        piece = alls[u].at[col_at, row_at, chunk_at]
        for d in range(1, regions):
            send(owns, remote(piece, piece, s3.at[u, d - 1], r3.at[u, chunk_at], along[d - 1]))

    def gather_regions(u):
        def arrive(d):
            chunk = lax.rem(chunk_at + d, CHUNKS)
            piece = alls[u].at[col_at, row_at, chunk]
            remote(piece, piece, s3.at[u, 0], r3.at[u, chunk], partner).wait_recv()

        for d in range(1, CHUNKS):
            arrive(d)
        if stride > 1:
            guarded(jnp.logical_not(owner), lambda: arrive(0))
        own = block(u, col_at, row_at)
        for d, peer in enumerate(across):
            send(True, remote(own, own, s4.at[u, d], r4.at[u, col_at], peer))
        send(True, remote(own, own, s5.at[u, 0], r5.at[u, col_at], partner))

    def gather_cols(u):
        for d, col in enumerate(cols):
            piece = block(u, col, row_at)
            remote(piece, piece, s4.at[u, d], r4.at[u, col], partner).wait_recv()
            send(True, remote(piece, piece, s5.at[u, d + 1], r5.at[u, col], partner))

    def gather_cores(u):
        for d in range(IMAGES):
            col = lax.rem(col_at + d, IMAGES)
            piece = block(u, col, 1 - row_at)
            remote(piece, piece, s5.at[u, d], r5.at[u, col], partner).wait_recv()

    for u in range(count):
        reduce_cores(u)
    for u in range(count):
        reduce_regions(u)
    for u in range(count):
        gather_regions(u)
    for u in range(count):
        gather_cols(u)
    for u in range(count):
        gather_cores(u)
    for when, copy in sent:
        guarded(when, lambda: copy.wait_send())


def exchange(parts, regions, params):
    shapes = unit_shapes(params)
    count = len(shapes)
    dma = pltpu.SemaphoreType.DMA
    vmem = pl.BlockSpec(memory_space=pltpu.VMEM)
    return pl.pallas_call(
        functools.partial(exchange_kernel, regions, params),
        out_shape=[jax.ShapeDtypeStruct((IMAGES,) + s, jnp.float32) for s in shapes],
        in_specs=[vmem] * count,
        out_specs=[vmem] * count,
        scratch_shapes=[pltpu.VMEM(s[1:], jnp.float32) for s in shapes]
        + [pltpu.VMEM(s[1:], jnp.float32) for s in shapes]
        + [pltpu.VMEM((regions - 1,) + s[2:], jnp.float32) for s in shapes]
        + [
            dma((count,)),
            dma((count,)),
            dma((count, CHUNKS)),
            dma((count, regions - 1)),
            dma((count, regions - 1)),
            dma((count, CHUNKS)),
            dma((count, IMAGES - 1)),
            dma((count, IMAGES)),
            dma((count, IMAGES)),
            dma((count, IMAGES)),
        ],
        compiler_params=pltpu.CompilerParams(
            collective_id=0, has_side_effects=True, vmem_limit_bytes=VMEM_LIMIT
        ),
        name="exchange",
    )(*parts)


def split(x):
    high = x.astype(jnp.bfloat16)
    return high, (x - high.astype(jnp.float32)).astype(jnp.bfloat16)


def product(left, right):
    lh, ll = left
    rh, rl = right
    dot = functools.partial(lax.dot_general, dimension_numbers=NT, preferred_element_type=jnp.float32)
    return dot(lh, rh) + (dot(ll, rh) + dot(lh, rl))


def eliminate(tile):
    shape = (8, TILE)
    sub = lax.broadcasted_iota(jnp.int32, shape, 0)
    lane = lax.broadcasted_iota(jnp.int32, shape, 1)
    other = sub + 1 - 2 * lax.rem(sub, 2)
    zero = jnp.zeros(shape, jnp.float32)
    count = TILE // 8
    f = [tile[8 * i : 8 * i + 8, :] for i in range(count)]

    def swap(x):
        return jnp.take_along_axis(x, other, axis=0, mode="promise_in_bounds")

    def down(x, p):
        return jnp.broadcast_to(x[p : p + 1, :], shape)

    def along(x, l):
        return jnp.broadcast_to(x[:, l : l + 1], shape)

    for g in range(TILE // GROUP):
        j = GROUP * g
        c = [[along(f[2 * g + h], j + s) for h in range(2)] for s in range(GROUP)]
        inside = (lane >= j) & (lane < j + GROUP)
        rows = [
            jnp.where(inside, (lane - j == sub + 8 * h).astype(jnp.float32), f[2 * g + h]) for h in range(2)
        ]
        main, cross, lower, scale = ([zero, zero] for _ in range(4))
        for p in range(0, GROUP, 2):
            h0, q0 = p // 8, p % 8
            cp, cq = list(c[p]), list(c[p + 1])
            a, b, d = down(cp[h0], q0), down(cp[h0], q0 + 1), down(cq[h0], q0 + 1)
            det = a * d - b * b
            inv = 1.0 / det
            left = [h for h in range(h0, 2) if 8 * h + 7 > p + 1]
            u, v = {}, {}
            for h in left:
                u[h] = d * cp[h] - b * cq[h]
                v[h] = a * cq[h] - b * cp[h]
                if 8 * h <= p + 1:
                    u[h] = jnp.where(sub > q0 + 1, u[h], 0.0)
                    v[h] = jnp.where(sub > q0 + 1, v[h], 0.0)
            ui = {h: u[h] * inv for h in left}
            vi = {h: v[h] * inv for h in left}
            for s in range(p + 2, GROUP):
                cs, ct = down(cp[s // 8], s % 8), down(cq[s // 8], s % 8)
                for h in left:
                    if s < p + 4:
                        c[s][h] = c[s][h] - (u[h] * cs + v[h] * ct) * inv
                    else:
                        c[s][h] = c[s][h] - ui[h] * cs - vi[h] * ct
            rp, rq = down(rows[h0], q0), down(rows[h0], q0 + 1)
            for h in left:
                rows[h] = rows[h] - ui[h] * rp - vi[h] * rq
            ia = 1.0 / a
            m0, m1 = sub == q0, sub == q0 + 1
            main[h0] = jnp.where(m0, d * inv, jnp.where(m1, a * inv, main[h0]))
            cross[h0] = jnp.where(m0 | m1, b * inv, cross[h0])
            lower[h0] = jnp.where(m1, b * ia, lower[h0])
            scale[h0] = jnp.where(m0, ia, jnp.where(m1, a * inv, scale[h0]))

        def pairs(x, h):
            return main[h] * x - cross[h] * swap(x)

        w = [pairs(rows[h], h) for h in range(2)]
        for q in range(GROUP - 2, 0, -2):
            wq = [down(w[q // 8], q % 8 + t) for t in range(2)]
            for h in range((q - 1) // 8 + 1):
                for t in range(2):
                    l = pairs(c[q + t][h], h)
                    if 8 * h + 8 > q:
                        l = jnp.where(sub < q - 8 * h, l, 0.0)
                    w[h] = w[h] - l * wq[t]
        near = min(count, 2 * g + 4)
        if near < count:
            far = jnp.concatenate(f[near:], axis=0)
            wide = [zero] * count
            wide[2 * g], wide[2 * g + 1] = w
            update = jnp.dot(
                far,
                jnp.concatenate(wide, axis=0),
                precision=lax.Precision.HIGHEST,
                preferred_element_type=jnp.float32,
            )
        spread = [down(w[p // 8], p % 8) for p in range(GROUP)]
        for i in range(2 * g + 2, near):
            value = jnp.where(inside, 0.0, f[i])
            for p in reversed(range(GROUP)):
                value = value - along(f[i], j + p) * spread[p]
            f[i] = value
        for i in range(near, count):
            f[i] = jnp.where(inside, 0.0, f[i]) - update[8 * (i - near) : 8 * (i - near) + 8]
        for h in range(2):
            f[2 * g + h] = (rows[h] - lower[h] * swap(rows[h])) * jnp.sqrt(scale[h])
    return jnp.concatenate([jnp.where(lane <= sub + 8 * i, f[i], 0.0) for i in range(count)], axis=0)


def factor_kernel(params, *refs):
    us = units(params)
    alls, refs = refs[: len(us)], refs[len(us) :]
    factor_ref, solved_ref, a_ref, linv_ref, high_ref, low_ref = refs
    total = IMAGES * params
    own = params // 4
    half = params // 2
    a_ref[total : total + EXTRA, :] = jnp.zeros((EXTRA, total), jnp.float32)
    for all_ref, (b, c0, w) in zip(alls, us):
        left = b * params + c0
        for col in range(IMAGES):
            for core in range(2):
                for q in range(CHUNKS):
                    for a in range(IMAGES - b):
                        row = (a + b) * params + col * own + (core * CHUNKS + q) * ROWS
                        a_ref[row : row + ROWS, left : left + w] = all_ref[
                            col, core, q, a * ROWS : (a + 1) * ROWS, :
                        ]
        if c0 + w == params:
            for t in range(2):
                at = b * params + t * half
                a_ref[total : total + 1, at : at + half] = all_ref[0, 0, 0, t : t + 1, w - half : w]
    panels = total // TILE
    eye_r = lax.broadcasted_iota(jnp.int32, (TILE, TILE), 0)
    eye_c = lax.broadcasted_iota(jnp.int32, (TILE, TILE), 1)
    damp = jnp.where(eye_r == eye_c, damping, 0.0).astype(jnp.float32)

    def panel(n, _):
        at = pl.ds(pl.multiple_of(n * TILE, TILE), TILE)
        tile = a_ref[at, at] + damp
        a_ref[at, at] = tile
        linv_ref[...] = eliminate(tile)
        for s in range(panels):

            @pl.when(n == s)
            def _():
                lo = s * TILE
                hi = lo + TILE
                end = total + EXTRA
                below = product(split(a_ref[lo:end, lo:hi]), split(linv_ref[...]))
                a_ref[lo:end, lo:hi] = below
                high, low = split(below)
                high_ref[lo:end, 0:TILE] = high
                high_ref[lo:end, TILE : 2 * TILE] = low
                low_ref[lo:end, 0:TILE] = high
                low_ref[lo:end, TILE : 2 * TILE] = high
                col = hi
                while col < total:
                    width = 2 * TILE if col % (2 * TILE) == 0 else TILE
                    dot = functools.partial(
                        lax.dot_general, dimension_numbers=NT, preferred_element_type=jnp.float32
                    )
                    a_ref[col:end, col : col + width] -= dot(
                        high_ref[col:end, :], low_ref[col : col + width, :]
                    ) + dot(high_ref[col:end, 0:TILE], high_ref[col : col + width, TILE : 2 * TILE])
                    col += width

        return 0

    lax.fori_loop(0, panels, panel, 0)
    row_block = factor_ref.shape[0]
    first_row = pl.multiple_of(
        (lax.axis_index("region") * 2 + lax.axis_index("row")) * row_block, row_block
    )
    first_col = pl.multiple_of(lax.axis_index("col") * params, params)
    held = a_ref[pl.ds(first_row, row_block), pl.ds(first_col, params)]
    at_row = first_row + lax.broadcasted_iota(jnp.int32, held.shape, 0)
    at_col = first_col + lax.broadcasted_iota(jnp.int32, held.shape, 1)
    factor_ref[...] = jnp.where(at_row >= at_col, held, 0.0)
    solved_ref[...] = a_ref[total, :]


def factorize(everything, params, row_block):
    total = IMAGES * params
    vmem = pl.BlockSpec(memory_space=pltpu.VMEM)
    return pl.pallas_call(
        functools.partial(factor_kernel, params),
        out_shape=(
            jax.ShapeDtypeStruct((row_block, params), jnp.float32),
            jax.ShapeDtypeStruct((total,), jnp.float32),
        ),
        in_specs=[vmem] * len(everything),
        out_specs=(vmem, vmem),
        scratch_shapes=[
            pltpu.VMEM((total + EXTRA, total), jnp.float32),
            pltpu.VMEM((TILE, TILE), jnp.float32),
            pltpu.VMEM((total + EXTRA, 2 * TILE), jnp.bfloat16),
            pltpu.VMEM((total + EXTRA, 2 * TILE), jnp.bfloat16),
        ],
        compiler_params=pltpu.CompilerParams(vmem_limit_bytes=VMEM_LIMIT),
        name="factorize",
    )(*everything)


def on_device(cam_jac, point_rows, track_images, track_counts):
    regions = lax.axis_size("region")
    params = cam_jac.shape[2]
    row_block = IMAGES * params // (regions * lax.axis_size("row"))
    parts = accumulate(cam_jac, point_rows, track_images, track_counts)
    everything = exchange(parts, regions, params)
    factor, solved = factorize(everything, params, row_block)
    return (factor, solved)


def solution(mesh):
    in_specs = (
        P(None, None, None, "region"),
        P(None, None, None, "region"),
        P(None, "region"),
        P(),
    )
    out_specs = (P(("region", "row"), "col"), P())
    return jax.shard_map(
        on_device, mesh=mesh, in_specs=in_specs, out_specs=out_specs, check_vma=False
    )
```

```python
import functools

import jax
import jax.numpy as jnp
from jax import lax
from jax.experimental import pallas as pl
from jax.experimental.pallas import tpu as pltpu
from jax.sharding import PartitionSpec as P

IMAGES = 4
CHUNKS = 4
ROWS = 8
BLOCK = 512
TILE = 128
GROUP = 16
EXTRA = 16
VMEM_LIMIT = 60 * 1024 * 1024

damping = 0.1
point_damping = 0.5

NT = (((1,), (1,)), ((), ()))
MESH = pl.DeviceIdType.MESH


def point_terms(pts):
    views = len(pts)
    pairs = [(k, r) for k in range(views) for r in range(2)]

    def entry(left, right):
        return sum(pts[k][r][left] * pts[k][r][right] for k, r in pairs)

    d1 = jnp.sqrt(entry(0, 0) + point_damping)
    b1 = entry(1, 0) / d1
    bf = entry(2, 0) / d1
    d2 = jnp.sqrt(entry(1, 1) + point_damping - b1 * b1)
    b2 = (entry(2, 1) - bf * b1) / d2
    d3 = jnp.sqrt(entry(2, 2) + point_damping - bf * bf - b2 * b2)

    def solve(first, second, third):
        o1 = first / d1
        o2 = (second - b1 * o1) / d2
        o3 = (third - bf * o1 - b2 * o2) / d3
        return [o.astype(jnp.bfloat16).astype(jnp.float32) for o in (o1, o2, o3)]

    coef = {(k, r): solve(*pts[k][r][0:3]) for k, r in pairs}
    step = solve(*[entry(c, 3) for c in range(3)])
    return coef, step


def part_at(u):
    return u // 2, u % 2 == 0


def part_shapes(params):
    shapes = []
    for u in range(2 * IMAGES - 1):
        b, diagonal = part_at(u)
        tail = (ROWS, params) if diagonal else ((IMAGES - 1 - b) * 2 * ROWS, params // 2)
        shapes.append((2, CHUNKS) + tail)
    return shapes


def accumulate_kernel(block, pos_ref, cam_ref, pts_ref, img_ref, *refs):
    params=cam_ref.shape[2]
    count_out=2*IMAGES-1
    outs=refs[:count_out]; refs=refs[count_out:]
    accs=refs[:IMAGES]; rhs=refs[IMAGES:2*IMAGES]; lhs=refs[2*IMAGES:3*IMAGES]
    views=cam_ref.shape[0]
    own=params//4
    step=pl.program_id(0)
    count=pos_ref[lax.axis_index("region")]
    row_at=lax.axis_index("row"); col_at=lax.axis_index("col")
    start=(2*step+row_at)*block
    sub=16
    @pl.when(step==0)
    def _():
        for a in accs: a[...]=jnp.zeros_like(a)
    @pl.when(start<count)
    def _():
        slot=start+lax.broadcasted_iota(jnp.int32,(1,block),1)
        live=slot<count
        pts=[]
        for k in range(views):
            pts.append([])
            for r in range(2):
                wide=pts_ref[k,r].astype(jnp.float32)
                pts[k].append([wide[c:c+1,:] for c in range(4)])
        coef,y=point_terms(pts)
        images=[img_ref[k:k+1,:] for k in range(views)]
        zero=jnp.zeros((sub-2,block),jnp.float32)
        def pick(masks,values):
            out=jnp.zeros_like(values[0])
            for mask,value in zip(masks,values): out=jnp.where(mask,value,out)
            return out
        def widen(mask):
            return jnp.broadcast_to(mask.astype(jnp.float32),(sub,block)).astype(jnp.bfloat16)>0
        masks=[[(images[k]==a)&live for k in range(views)] for a in range(IMAGES)]
        wide=[[widen(m) for m in masks[a][:2]] for a in range(IMAGES)]
        c=[[[pick(masks[a],[coef[k,r][m] for k in range(views)]) for m in range(3)] for r in range(2)] for a in range(IMAGES)]
        held=[(masks[a][0]|masks[a][1]|masks[a][2]).astype(jnp.float32) for a in range(IMAGES)]
        err=[[pick(masks[a],[pts[k][r][3] for k in range(views)]) for r in range(2)] for a in range(IMAGES)]
        def chosen(a,at,r):
            j=[cam_ref[k,r,pl.ds(at,sub),:] for k in range(views)]
            return jnp.where(wide[a][0],j[0],jnp.where(wide[a][1],j[1],j[2]))
        mine=pl.multiple_of(col_at*own,own)
        for b in range(IMAGES):
            for i in range(params//sub):
                for r in range(2):
                    rhs[b][i*sub:(i+1)*sub,r*block:(r+1)*block]=chosen(b,i*sub,r)
            for a in range(b,IMAGES):
                x={}
                for r in range(2):
                    for s in range(2):
                        if a==b and s<r: x[r,s]=x[s,r]; continue
                        v=-(c[a][r][0]*c[b][s][0]+c[a][r][1]*c[b][s][1]+c[a][r][2]*c[b][s][2])
                        x[r,s]=v+held[a] if a==b and r==s else v
                for i in range(own//sub):
                    jac=[chosen(a,mine+i*sub,r).astype(jnp.float32) for r in range(2)]
                    for s in range(2):
                        v=jac[0]*x[0,s]+jac[1]*x[1,s]
                        lhs[b][(a-b)*own+i*sub:(a-b)*own+(i+1)*sub,s*block:(s+1)*block]=v.astype(jnp.bfloat16)
            depth=(IMAGES-b)*own
            for r in range(2):
                g=err[b][r]-(c[b][r][0]*y[0]+c[b][r][1]*y[1]+c[b][r][2]*y[2])
                near=g.astype(jnp.bfloat16).astype(jnp.float32)
                lhs[b][depth:depth+sub,r*block:(r+1)*block]=jnp.concatenate([near,g-near,zero],axis=0).astype(jnp.bfloat16)
            accs[b][...]+=lax.dot_general(lhs[b][...],rhs[b][...],NT,preferred_element_type=jnp.float32)
    @pl.when(step==pl.num_programs(0)-1)
    def _():
        half=params//2
        for b in range(IMAGES):
            acc=accs[b]
            depth=(IMAGES-b)*own
            sub8=lax.broadcasted_iota(jnp.int32,(8,half),0)
            grad=acc[depth:depth+1,:]+acc[depth+1:depth+2,:]
            one=jnp.broadcast_to(grad[:,0:half],(8,half))
            two=jnp.broadcast_to(grad[:,half:params],(8,half))
            held=acc[0:8,half:params]
            grad=jnp.where(sub8==0,one,jnp.where(sub8==1,two,held))
            acc[0:8,half:params]=jnp.where(col_at==0,grad,held)
        for u, out in enumerate(outs):
            b, diagonal = part_at(u)
            acc = accs[b]
            for core in range(2):
                for q in range(CHUNKS):
                    if diagonal:
                        src = (core * CHUNKS + q) * ROWS
                        out[core, q] = acc[src : src + ROWS, :]
                    else:
                        wide = 2 * ROWS
                        at = q % 2 * half
                        for i in range(IMAGES - 1 - b):
                            src = (i + 1) * own + (core * 2 + q // 2) * wide
                            out[core, q, i * wide : (i + 1) * wide, :] = acc[src : src + wide, at : at + half]


def accumulate(cam_jac,point_rows,track_images,pos,block=BLOCK):
    views,_,params,slots=cam_jac.shape
    own=params//4
    block=min(block,slots//2)
    def at(i,p):
        return jnp.minimum(2*i+lax.axis_index("row"),(p[lax.axis_index("region")]-1)//block)
    shapes=part_shapes(params)
    return pl.pallas_call(
        functools.partial(accumulate_kernel, block),
        out_shape=[jax.ShapeDtypeStruct(s,jnp.float32) for s in shapes],
        grid_spec=pltpu.PrefetchScalarGridSpec(
            num_scalar_prefetch=1, grid=(slots//block//2,),
            in_specs=[pl.BlockSpec((views,2,params,block),lambda i,p:(0,0,0,at(i,p))),
                      pl.BlockSpec((views,2,4,block),lambda i,p:(0,0,0,at(i,p))),
                      pl.BlockSpec((views,block),lambda i,p:(0,at(i,p)))],
            out_specs=[pl.BlockSpec(s,lambda i,p:(0,0,0,0)) for s in shapes],
            scratch_shapes=[pltpu.VMEM(((IMAGES-b)*own+16,params),jnp.float32) for b in range(IMAGES)]+[
                pltpu.VMEM((params,2*block),jnp.bfloat16) for b in range(IMAGES)]+[
                pltpu.VMEM(((IMAGES-b)*own+16,2*block),jnp.bfloat16) for b in range(IMAGES)]),
        compiler_params=pltpu.CompilerParams(dimension_semantics=("arbitrary",),vmem_limit_bytes=VMEM_LIMIT),
        name="accumulate")(pos,cam_jac,point_rows,track_images)


def split(x):
    high = x.astype(jnp.bfloat16)
    return high, (x - high.astype(jnp.float32)).astype(jnp.bfloat16)


def product(left, right):
    lh, ll = left
    rh, rl = right
    dot = functools.partial(lax.dot_general, dimension_numbers=NT, preferred_element_type=jnp.float32)
    return dot(lh, rh) + (dot(ll, rh) + dot(lh, rl))


def eliminate(tile):
    shape = (8, TILE)
    sub = lax.broadcasted_iota(jnp.int32, shape, 0)
    lane = lax.broadcasted_iota(jnp.int32, shape, 1)
    other = sub + 1 - 2 * lax.rem(sub, 2)
    zero = jnp.zeros(shape, jnp.float32)
    count = TILE // 8
    f = [tile[8 * i : 8 * i + 8, :] for i in range(count)]

    def swap(x):
        return jnp.take_along_axis(x, other, axis=0, mode="promise_in_bounds")

    def down(x, p):
        return jnp.broadcast_to(x[p : p + 1, :], shape)

    def along(x, l):
        return jnp.broadcast_to(x[:, l : l + 1], shape)

    for g in range(TILE // GROUP):
        j = GROUP * g
        c = [[along(f[2 * g + h], j + s) for h in range(2)] for s in range(GROUP)]
        inside = (lane >= j) & (lane < j + GROUP)
        rows = [
            jnp.where(inside, (lane - j == sub + 8 * h).astype(jnp.float32), f[2 * g + h]) for h in range(2)
        ]
        main, cross, lower, scale = ([zero, zero] for _ in range(4))
        for p in range(0, GROUP, 2):
            h0, q0 = p // 8, p % 8
            cp, cq = list(c[p]), list(c[p + 1])
            a, b, d = down(cp[h0], q0), down(cp[h0], q0 + 1), down(cq[h0], q0 + 1)
            det = a * d - b * b
            inv = 1.0 / det
            left = [h for h in range(h0, 2) if 8 * h + 7 > p + 1]
            u, v = {}, {}
            for h in left:
                u[h] = d * cp[h] - b * cq[h]
                v[h] = a * cq[h] - b * cp[h]
                if 8 * h <= p + 1:
                    u[h] = jnp.where(sub > q0 + 1, u[h], 0.0)
                    v[h] = jnp.where(sub > q0 + 1, v[h], 0.0)
            ui = {h: u[h] * inv for h in left}
            vi = {h: v[h] * inv for h in left}
            for s in range(p + 2, GROUP):
                cs, ct = down(cp[s // 8], s % 8), down(cq[s // 8], s % 8)
                for h in left:
                    if s < p + 4:
                        c[s][h] = c[s][h] - (u[h] * cs + v[h] * ct) * inv
                    else:
                        c[s][h] = c[s][h] - ui[h] * cs - vi[h] * ct
            rp, rq = down(rows[h0], q0), down(rows[h0], q0 + 1)
            for h in left:
                rows[h] = rows[h] - ui[h] * rp - vi[h] * rq
            ia = 1.0 / a
            m0, m1 = sub == q0, sub == q0 + 1
            main[h0] = jnp.where(m0, d * inv, jnp.where(m1, a * inv, main[h0]))
            cross[h0] = jnp.where(m0 | m1, b * inv, cross[h0])
            lower[h0] = jnp.where(m1, b * ia, lower[h0])
            scale[h0] = jnp.where(m0, ia, jnp.where(m1, a * inv, scale[h0]))

        def pairs(x, h):
            return main[h] * x - cross[h] * swap(x)

        w = [pairs(rows[h], h) for h in range(2)]
        for q in range(GROUP - 2, 0, -2):
            wq = [down(w[q // 8], q % 8 + t) for t in range(2)]
            for h in range((q - 1) // 8 + 1):
                for t in range(2):
                    l = pairs(c[q + t][h], h)
                    if 8 * h + 8 > q:
                        l = jnp.where(sub < q - 8 * h, l, 0.0)
                    w[h] = w[h] - l * wq[t]
        near = min(count, 2 * g + 4)
        if near < count:
            far = jnp.concatenate(f[near:], axis=0)
            wide = [zero] * count
            wide[2 * g], wide[2 * g + 1] = w
            update = jnp.dot(
                far,
                jnp.concatenate(wide, axis=0),
                precision=lax.Precision.HIGHEST,
                preferred_element_type=jnp.float32,
            )
        spread = [down(w[p // 8], p % 8) for p in range(GROUP)]
        for i in range(2 * g + 2, near):
            value = jnp.where(inside, 0.0, f[i])
            for p in reversed(range(GROUP)):
                value = value - along(f[i], j + p) * spread[p]
            f[i] = value
        for i in range(near, count):
            f[i] = jnp.where(inside, 0.0, f[i]) - update[8 * (i - near) : 8 * (i - near) + 8]
        for h in range(2):
            f[2 * g + h] = (rows[h] - lower[h] * swap(rows[h])) * jnp.sqrt(scale[h])
    return jnp.concatenate([jnp.where(lane <= sub + 8 * i, f[i], 0.0) for i in range(count)], axis=0)


def finish_kernel(regions, params, *refs):
    shapes = part_shapes(params)
    count = len(shapes)
    parts, refs = refs[:count], refs[count:]
    factor_ref, solved_ref = refs[:2]
    refs = refs[2:]
    alls, refs = refs[:count], refs[count:]
    recv1, refs = refs[:count], refs[count:]
    mine, refs = refs[:count], refs[count:]
    recv2, refs = refs[:count], refs[count:]
    a_ref, linv_ref, high_ref, low_ref = refs[:4]
    s1, r1, s2, r2, s3, r3, s4, r4, s5, r5, s6, r6 = refs[4:]
    total = IMAGES * params
    own = params // 4
    half = params // 2
    stride = regions // CHUNKS
    region_at = lax.axis_index("region")
    row_at = lax.axis_index("row")
    col_at = lax.axis_index("col")
    chunk_at = region_at // stride
    owner = lax.rem(region_at, stride) == 0
    other = lax.rem(region_at, stride) != 0

    def device(region, row, col):
        return {"region": region, "row": row, "col": col}

    def remote(src, dst, send, recv, to):
        return pltpu.make_async_remote_copy(
            src_ref=src, dst_ref=dst, send_sem=send, recv_sem=recv, device_id=to, device_id_type=MESH
        )

    def landed(ref, recv):
        remote(ref, ref, s1.at[0], recv, partner).wait_recv()

    def guarded(when, action):
        if when is True:
            action()
        else:
            pl.when(when)(action)

    owns = True if stride == 1 else owner
    partner = device(region_at, 1 - row_at, col_at)
    along = [device(lax.rem(region_at + d, regions), row_at, col_at) for d in range(1, regions)]
    cols = [lax.rem(col_at + d, IMAGES) for d in range(IMAGES)]
    across = [device(region_at, row_at, c) for c in cols[1:]]
    others = [
        device(lax.rem(region_at + d, regions), row_at, cols[e])
        for d in range(regions)
        for e in range(IMAGES)
        if d + e > 0
    ]
    barrier = pltpu.get_barrier_semaphore()
    for peer in [partner] + others:
        pl.semaphore_signal(barrier, inc=1, device_id=peer, device_id_type=MESH)
    pl.semaphore_wait(barrier, 1 + len(others))
    sent = []

    def send(when, src, dst, sems, index, recv, to, like):
        sent.append((when, like, sems, index))
        guarded(when, lambda: remote(src, dst, sems.at[index], recv, to).start())

    def swap_cores(u):
        send(True, parts[u].at[1 - row_at], recv1[u], s1, (u,), r1.at[u], partner, lambda: recv1[u])

    def reduce_cores(u):
        landed(recv1[u], r1.at[u])
        mine[u][...] = (parts[u][row_at] + recv1[u][...]).astype(mine[u].dtype)
        for d in range(0 if stride > 1 else 1, CHUNKS):
            chunk = lax.rem(chunk_at + d, CHUNKS)
            to = chunk * stride
            gap = lax.rem(to - region_at + regions, regions)
            send(
                True if d else other,
                mine[u].at[chunk],
                recv2[u].at[gap - 1],
                s2,
                (u, d),
                r2.at[u, gap - 1],
                device(to, row_at, col_at),
                lambda: mine[u].at[0],
            )

    def reduce_regions(u):
        def add():
            value = mine[u][chunk_at].astype(jnp.float32)
            for gap in range(regions - 1):
                landed(recv2[u].at[gap], r2.at[u, gap])
                value = value + recv2[u][gap].astype(jnp.float32)
            alls[u][col_at, row_at, chunk_at] = value.astype(alls[u].dtype)

        guarded(owns, add)
        piece = alls[u].at[col_at, row_at, chunk_at]
        if u == 0:
            for i, peer in enumerate(others):
                send(owns, piece, piece, s6, (i,), r6.at[col_at, chunk_at], peer, lambda: mine[u].at[0])
        else:
            for d, peer in enumerate(along):
                send(owns, piece, piece, s3, (u, d,), r3.at[u, chunk_at], peer, lambda: mine[u].at[0])

    def forward(u, d):
        piece = alls[u].at[cols[d], row_at]
        send(True, piece, piece, s5, (u, d,), r5.at[u, cols[d]], partner, lambda: mine[u])

    def gather_regions(u):
        def arrive(e, d):
            chunk = lax.rem(chunk_at + d, CHUNKS)
            landed(alls[u].at[cols[e], row_at, chunk], r6.at[cols[e], chunk] if u == 0 else r3.at[u, chunk])

        for e in range(IMAGES if u == 0 else 1):
            for d in range(CHUNKS):
                if d + e > 0:
                    arrive(e, d)
                elif stride > 1:
                    guarded(other, lambda: arrive(0, 0))
            forward(u, e)
        if u > 0:
            piece = alls[u].at[col_at, row_at]
            for d, peer in enumerate(across):
                send(True, piece, piece, s4, (u, d,), r4.at[u, col_at], peer, lambda: mine[u])

    def gather_cols(u):
        for d in range(1, IMAGES):
            landed(alls[u].at[cols[d], row_at], r4.at[u, cols[d]])
            forward(u, d)

    def place(u):
        for d in range(IMAGES):
            landed(alls[u].at[cols[d], 1 - row_at], r5.at[u, cols[d]])
        b, diagonal = part_at(u)
        left = b * params
        for col in range(IMAGES):
            for core in range(2):
                for q in range(CHUNKS):
                    value = alls[u][col, core, q].astype(jnp.float32)
                    if diagonal:
                        row = b * params + col * own + (core * CHUNKS + q) * ROWS
                        a_ref[row : row + ROWS, left : left + params] += value
                    else:
                        wide = 2 * ROWS
                        at = left + q % 2 * half
                        for i in range(IMAGES - 1 - b):
                            row = (b + 1 + i) * params + col * own + (core * 2 + q // 2) * wide
                            a_ref[row : row + wide, at : at + half] += value[i * wide : (i + 1) * wide]
        if diagonal:
            for t in range(2):
                at = left + t * half
                a_ref[total : total + 1, at : at + half] += alls[u][0, 0, 0, t : t + 1, half:params]

    for u in range(count):
        swap_cores(u)
    a_ref[...] = jnp.zeros_like(a_ref)
    reduce_cores(0)
    reduce_cores(1)
    reduce_regions(0)
    reduce_cores(2)
    reduce_cores(3)
    reduce_regions(1)
    gather_regions(0)
    reduce_regions(2)
    gather_regions(1)
    reduce_regions(3)
    place(0)

    def at_panel(s):
        before, after = {
            0: (
                [(gather_cols, 1), (gather_regions, 2), (place, 1), (gather_regions, 3)],
                [(reduce_cores, 4), (reduce_cores, 5)],
            ),
            1: ([], [(gather_cols, 2), (reduce_regions, 4), (reduce_regions, 5), (place, 2)]),
            2: ([(gather_cols, 3), (reduce_cores, 6), (place, 3)], [(gather_regions, 4), (gather_regions, 5)]),
            3: ([], [(gather_cols, 4), (reduce_regions, 6), (place, 4)]),
            4: ([(gather_cols, 5), (place, 5)], [(gather_regions, 6)]),
            5: ([], [(gather_cols, 6), (place, 6)]),
        }.get(s, ([], []))
        return before, after

    panels = total // TILE
    eye_r = lax.broadcasted_iota(jnp.int32, (TILE, TILE), 0)
    eye_c = lax.broadcasted_iota(jnp.int32, (TILE, TILE), 1)
    damp = jnp.where(eye_r == eye_c, damping, 0.0).astype(jnp.float32)
    dot = functools.partial(lax.dot_general, dimension_numbers=NT, preferred_element_type=jnp.float32)

    def panel(n, _):
        at = pl.ds(pl.multiple_of(n * TILE, TILE), TILE)
        tile = a_ref[at, at] + damp
        a_ref[at, at] = tile
        linv_ref[...] = eliminate(tile)
        for s in range(panels):

            @pl.when(n == s)
            def _():
                before, after = at_panel(s)
                for action, u in before:
                    action(u)
                lo = s * TILE
                hi = lo + TILE
                end = total + EXTRA
                below = product(split(a_ref[lo:end, lo:hi]), split(linv_ref[...]))
                a_ref[lo:end, lo:hi] = below
                high, low = split(below)
                high_ref[lo:end, 0:TILE] = high
                high_ref[lo:end, TILE : 2 * TILE] = low
                low_ref[lo:end, 0:TILE] = high
                low_ref[lo:end, TILE : 2 * TILE] = high
                col = hi
                while col < total:
                    width = 2 * TILE if col % (2 * TILE) == 0 else TILE
                    a_ref[col:end, col : col + width] -= dot(
                        high_ref[col:end, :], low_ref[col : col + width, :]
                    ) + dot(high_ref[col:end, 0:TILE], high_ref[col : col + width, TILE : 2 * TILE])
                    col += width
                for action, u in after:
                    action(u)

        return 0

    lax.fori_loop(0, panels, panel, 0)
    for when, like, sems, index in sent:
        guarded(when, lambda: remote(like(), like(), sems.at[index], r1.at[0], partner).wait_send())
    row_block = factor_ref.shape[0]
    first_row = pl.multiple_of((region_at * 2 + row_at) * row_block, row_block)
    first_col = pl.multiple_of(col_at * params, params)
    held = a_ref[pl.ds(first_row, row_block), pl.ds(first_col, params)]
    at_row = first_row + lax.broadcasted_iota(jnp.int32, held.shape, 0)
    at_col = first_col + lax.broadcasted_iota(jnp.int32, held.shape, 1)
    factor_ref[...] = jnp.where(at_row >= at_col, held, 0.0)
    solved_ref[...] = a_ref[total, :]


def finish(parts, regions, params, row_block):
    shapes = part_shapes(params)
    count = len(shapes)
    types = [jnp.float32 if part_at(u)[1] else jnp.bfloat16 for u in range(count)]
    total = IMAGES * params
    dma = pltpu.SemaphoreType.DMA
    vmem = pl.BlockSpec(memory_space=pltpu.VMEM)
    peers = regions * IMAGES - 1
    return pl.pallas_call(
        functools.partial(finish_kernel, regions, params),
        out_shape=(
            jax.ShapeDtypeStruct((row_block, params), jnp.float32),
            jax.ShapeDtypeStruct((total,), jnp.float32),
        ),
        in_specs=[vmem] * count,
        out_specs=(vmem, vmem),
        scratch_shapes=[pltpu.VMEM((IMAGES,) + s, t) for s, t in zip(shapes, types)]
        + [pltpu.VMEM(s[1:], jnp.float32) for s in shapes]
        + [pltpu.VMEM(s[1:], t) for s, t in zip(shapes, types)]
        + [pltpu.VMEM((regions - 1,) + s[2:], t) for s, t in zip(shapes, types)]
        + [
            pltpu.VMEM((total + EXTRA, total), jnp.float32),
            pltpu.VMEM((TILE, TILE), jnp.float32),
            pltpu.VMEM((total + EXTRA, 2 * TILE), jnp.bfloat16),
            pltpu.VMEM((total + EXTRA, 2 * TILE), jnp.bfloat16),
            dma((count,)),
            dma((count,)),
            dma((count, CHUNKS)),
            dma((count, regions - 1)),
            dma((count, regions - 1)),
            dma((count, CHUNKS)),
            dma((count, IMAGES - 1)),
            dma((count, IMAGES)),
            dma((count, IMAGES)),
            dma((count, IMAGES)),
            dma((peers,)),
            dma((IMAGES, CHUNKS)),
        ],
        compiler_params=pltpu.CompilerParams(
            collective_id=0, has_side_effects=True, vmem_limit_bytes=VMEM_LIMIT
        ),
        name="finish",
    )(*parts)


def on_device(cam_jac, point_rows, track_images, track_counts):
    regions = lax.axis_size("region")
    params = cam_jac.shape[2]
    row_block = IMAGES * params // (regions * lax.axis_size("row"))
    parts = accumulate(cam_jac, point_rows, track_images, track_counts)
    factor, solved = finish(parts, regions, params, row_block)
    return (factor, solved)


def solution(mesh):
    in_specs = (
        P(None, None, None, "region"),
        P(None, None, None, "region"),
        P(None, "region"),
        P(),
    )
    out_specs = (P(("region", "row"), "col"), P())
    return jax.shard_map(
        on_device, mesh=mesh, in_specs=in_specs, out_specs=out_specs, check_vma=False
    )
```

```python
import functools

import jax
import jax.numpy as jnp
from jax import lax
from jax.experimental import pallas as pl
from jax.experimental.pallas import tpu as pltpu
from jax.sharding import PartitionSpec as P

IMAGES = 4
CHUNKS = 4
ROWS = 8
BLOCK = 512
TILE = 128
GROUP = 16
EXTRA = 16
VMEM_LIMIT = 60 * 1024 * 1024

damping = 0.1
point_damping = 0.5

NT = (((1,), (1,)), ((), ()))
NN = (((1,), (0,)), ((), ()))
MESH = pl.DeviceIdType.MESH


def point_terms(pts):
    views = len(pts)
    pairs = [(k, r) for k in range(views) for r in range(2)]

    def entry(left, right):
        return sum(pts[k][r][left] * pts[k][r][right] for k, r in pairs)

    d1 = jnp.sqrt(entry(0, 0) + point_damping)
    b1 = entry(1, 0) / d1
    bf = entry(2, 0) / d1
    d2 = jnp.sqrt(entry(1, 1) + point_damping - b1 * b1)
    b2 = (entry(2, 1) - bf * b1) / d2
    d3 = jnp.sqrt(entry(2, 2) + point_damping - bf * bf - b2 * b2)

    def solve(first, second, third):
        o1 = first / d1
        o2 = (second - b1 * o1) / d2
        o3 = (third - bf * o1 - b2 * o2) / d3
        return [o.astype(jnp.bfloat16).astype(jnp.float32) for o in (o1, o2, o3)]

    coef = {(k, r): solve(*pts[k][r][0:3]) for k, r in pairs}
    step = solve(*[entry(c, 3) for c in range(3)])
    return coef, step


def part_at(u):
    return u // 2, u % 2 == 0


def part_shapes(params):
    shapes = []
    for u in range(2 * IMAGES - 1):
        b, diagonal = part_at(u)
        tail = (ROWS, params) if diagonal else ((IMAGES - 1 - b) * 2 * ROWS, params // 2)
        shapes.append((2, CHUNKS) + tail)
    return shapes


def accumulate_kernel(block, pos_ref, cam_ref, pts_ref, img_ref, *refs):
    params=cam_ref.shape[2]
    count_out=2*IMAGES-1
    outs=refs[:count_out]; refs=refs[count_out:]
    accs=refs[:IMAGES]; rhs=refs[IMAGES:2*IMAGES]; lhs=refs[2*IMAGES:3*IMAGES]
    views=cam_ref.shape[0]
    own=params//4
    step=pl.program_id(0)
    count=pos_ref[lax.axis_index("region")]
    row_at=lax.axis_index("row"); col_at=lax.axis_index("col")
    start=(2*step+row_at)*block
    sub=16
    @pl.when(step==0)
    def _():
        for a in accs: a[...]=jnp.zeros_like(a)
    @pl.when(start<count)
    def _():
        slot=start+lax.broadcasted_iota(jnp.int32,(1,block),1)
        live=slot<count
        pts=[]
        for k in range(views):
            pts.append([])
            for r in range(2):
                wide=pts_ref[k,r].astype(jnp.float32)
                pts[k].append([wide[c:c+1,:] for c in range(4)])
        coef,y=point_terms(pts)
        images=[img_ref[k:k+1,:] for k in range(views)]
        zero=jnp.zeros((sub-2,block),jnp.float32)
        def pick(masks,values):
            out=jnp.zeros_like(values[0])
            for mask,value in zip(masks,values): out=jnp.where(mask,value,out)
            return out
        def widen(mask):
            return jnp.broadcast_to(mask.astype(jnp.float32),(sub,block)).astype(jnp.bfloat16)>0
        masks=[[(images[k]==a)&live for k in range(views)] for a in range(IMAGES)]
        wide=[[widen(m) for m in masks[a][:2]] for a in range(IMAGES)]
        c=[[[pick(masks[a],[coef[k,r][m] for k in range(views)]) for m in range(3)] for r in range(2)] for a in range(IMAGES)]
        held=[(masks[a][0]|masks[a][1]|masks[a][2]).astype(jnp.float32) for a in range(IMAGES)]
        err=[[pick(masks[a],[pts[k][r][3] for k in range(views)]) for r in range(2)] for a in range(IMAGES)]
        def chosen(a,at,r):
            j=[cam_ref[k,r,pl.ds(at,sub),:] for k in range(views)]
            return jnp.where(wide[a][0],j[0],jnp.where(wide[a][1],j[1],j[2]))
        mine=pl.multiple_of(col_at*own,own)
        for b in range(IMAGES):
            for i in range(params//sub):
                for r in range(2):
                    rhs[b][i*sub:(i+1)*sub,r*block:(r+1)*block]=chosen(b,i*sub,r)
            for a in range(b,IMAGES):
                x={}
                for r in range(2):
                    for s in range(2):
                        if a==b and s<r: x[r,s]=x[s,r]; continue
                        v=-(c[a][r][0]*c[b][s][0]+c[a][r][1]*c[b][s][1]+c[a][r][2]*c[b][s][2])
                        x[r,s]=v+held[a] if a==b and r==s else v
                for i in range(own//sub):
                    jac=[chosen(a,mine+i*sub,r).astype(jnp.float32) for r in range(2)]
                    for s in range(2):
                        v=jac[0]*x[0,s]+jac[1]*x[1,s]
                        lhs[b][(a-b)*own+i*sub:(a-b)*own+(i+1)*sub,s*block:(s+1)*block]=v.astype(jnp.bfloat16)
            depth=(IMAGES-b)*own
            for r in range(2):
                g=err[b][r]-(c[b][r][0]*y[0]+c[b][r][1]*y[1]+c[b][r][2]*y[2])
                near=g.astype(jnp.bfloat16).astype(jnp.float32)
                lhs[b][depth:depth+sub,r*block:(r+1)*block]=jnp.concatenate([near,g-near,zero],axis=0).astype(jnp.bfloat16)
            accs[b][...]+=lax.dot_general(lhs[b][...],rhs[b][...],NT,preferred_element_type=jnp.float32)
    @pl.when(step==pl.num_programs(0)-1)
    def _():
        half=params//2
        for b in range(IMAGES):
            acc=accs[b]
            depth=(IMAGES-b)*own
            sub8=lax.broadcasted_iota(jnp.int32,(8,half),0)
            grad=acc[depth:depth+1,:]+acc[depth+1:depth+2,:]
            one=jnp.broadcast_to(grad[:,0:half],(8,half))
            two=jnp.broadcast_to(grad[:,half:params],(8,half))
            held=acc[0:8,half:params]
            grad=jnp.where(sub8==0,one,jnp.where(sub8==1,two,held))
            acc[0:8,half:params]=jnp.where(col_at==0,grad,held)
        for u, out in enumerate(outs):
            b, diagonal = part_at(u)
            acc = accs[b]
            for core in range(2):
                for q in range(CHUNKS):
                    if diagonal:
                        src = (core * CHUNKS + q) * ROWS
                        out[core, q] = acc[src : src + ROWS, :]
                    else:
                        wide = 2 * ROWS
                        at = q % 2 * half
                        for i in range(IMAGES - 1 - b):
                            src = (i + 1) * own + (core * 2 + q // 2) * wide
                            out[core, q, i * wide : (i + 1) * wide, :] = acc[src : src + wide, at : at + half]


def accumulate(cam_jac,point_rows,track_images,pos,block=BLOCK):
    views,_,params,slots=cam_jac.shape
    own=params//4
    block=min(block,slots//2)
    def at(i,p):
        return jnp.minimum(2*i+lax.axis_index("row"),(p[lax.axis_index("region")]-1)//block)
    shapes=part_shapes(params)
    return pl.pallas_call(
        functools.partial(accumulate_kernel, block),
        out_shape=[jax.ShapeDtypeStruct(s,jnp.float32) for s in shapes],
        grid_spec=pltpu.PrefetchScalarGridSpec(
            num_scalar_prefetch=1, grid=(slots//block//2,),
            in_specs=[pl.BlockSpec((views,2,params,block),lambda i,p:(0,0,0,at(i,p))),
                      pl.BlockSpec((views,2,4,block),lambda i,p:(0,0,0,at(i,p))),
                      pl.BlockSpec((views,block),lambda i,p:(0,at(i,p)))],
            out_specs=[pl.BlockSpec(s,lambda i,p:(0,0,0,0)) for s in shapes],
            scratch_shapes=[pltpu.VMEM(((IMAGES-b)*own+16,params),jnp.float32) for b in range(IMAGES)]+[
                pltpu.VMEM((params,2*block),jnp.bfloat16) for b in range(IMAGES)]+[
                pltpu.VMEM(((IMAGES-b)*own+16,2*block),jnp.bfloat16) for b in range(IMAGES)]),
        compiler_params=pltpu.CompilerParams(dimension_semantics=("arbitrary",),vmem_limit_bytes=VMEM_LIMIT),
        name="accumulate")(pos,cam_jac,point_rows,track_images)


def split(x):
    high = x.astype(jnp.bfloat16)
    return high, (x - high.astype(jnp.float32)).astype(jnp.bfloat16)


def product(left, right, dims):
    lh, ll = left
    rh, rl = right
    dot = functools.partial(lax.dot_general, dimension_numbers=dims, preferred_element_type=jnp.float32)
    return dot(lh, rh) + (dot(ll, rh) + dot(lh, rl))


def eliminate(tile):
    shape = (8, TILE)
    sub = lax.broadcasted_iota(jnp.int32, shape, 0)
    lane = lax.broadcasted_iota(jnp.int32, shape, 1)
    other = sub + 1 - 2 * lax.rem(sub, 2)
    zero = jnp.zeros(shape, jnp.float32)
    count = TILE // 8
    f = [tile[8 * i : 8 * i + 8, :] for i in range(count)]

    def swap(x):
        return jnp.take_along_axis(x, other, axis=0, mode="promise_in_bounds")

    def down(x, p):
        return jnp.broadcast_to(x[p : p + 1, :], shape)

    def along(x, l):
        return jnp.broadcast_to(x[:, l : l + 1], shape)

    for g in range(TILE // GROUP):
        j = GROUP * g
        c = [[along(f[2 * g + h], j + s) for h in range(2)] for s in range(GROUP)]
        inside = (lane >= j) & (lane < j + GROUP)
        rows = [
            jnp.where(inside, (lane - j == sub + 8 * h).astype(jnp.float32), f[2 * g + h]) for h in range(2)
        ]
        main, cross, lower, scale = ([zero, zero] for _ in range(4))
        for p in range(0, GROUP, 2):
            h0, q0 = p // 8, p % 8
            cp, cq = list(c[p]), list(c[p + 1])
            a, b, d = down(cp[h0], q0), down(cp[h0], q0 + 1), down(cq[h0], q0 + 1)
            det = a * d - b * b
            inv = 1.0 / det
            left = [h for h in range(h0, 2) if 8 * h + 7 > p + 1]
            u, v = {}, {}
            for h in left:
                u[h] = d * cp[h] - b * cq[h]
                v[h] = a * cq[h] - b * cp[h]
                if 8 * h <= p + 1:
                    u[h] = jnp.where(sub > q0 + 1, u[h], 0.0)
                    v[h] = jnp.where(sub > q0 + 1, v[h], 0.0)
            ui = {h: u[h] * inv for h in left}
            vi = {h: v[h] * inv for h in left}
            for s in range(p + 2, GROUP):
                cs, ct = down(cp[s // 8], s % 8), down(cq[s // 8], s % 8)
                for h in left:
                    if s < p + 4:
                        c[s][h] = c[s][h] - (u[h] * cs + v[h] * ct) * inv
                    else:
                        c[s][h] = c[s][h] - ui[h] * cs - vi[h] * ct
            rp, rq = down(rows[h0], q0), down(rows[h0], q0 + 1)
            for h in left:
                rows[h] = rows[h] - ui[h] * rp - vi[h] * rq
            ia = 1.0 / a
            m0, m1 = sub == q0, sub == q0 + 1
            main[h0] = jnp.where(m0, d * inv, jnp.where(m1, a * inv, main[h0]))
            cross[h0] = jnp.where(m0 | m1, b * inv, cross[h0])
            lower[h0] = jnp.where(m1, b * ia, lower[h0])
            scale[h0] = jnp.where(m0, ia, jnp.where(m1, a * inv, scale[h0]))

        def pairs(x, h):
            return main[h] * x - cross[h] * swap(x)

        w = [pairs(rows[h], h) for h in range(2)]
        for q in range(GROUP - 2, 0, -2):
            wq = [down(w[q // 8], q % 8 + t) for t in range(2)]
            for h in range((q - 1) // 8 + 1):
                for t in range(2):
                    l = pairs(c[q + t][h], h)
                    if 8 * h + 8 > q:
                        l = jnp.where(sub < q - 8 * h, l, 0.0)
                    w[h] = w[h] - l * wq[t]
        near = min(count, 2 * g + 4)
        if near < count:
            far = jnp.concatenate(f[near:], axis=0)
            wide = [zero] * count
            wide[2 * g], wide[2 * g + 1] = w
            update = product(split(far), split(jnp.concatenate(wide, axis=0)), NN)
        spread = [down(w[p // 8], p % 8) for p in range(GROUP)]
        for i in range(2 * g + 2, near):
            value = jnp.where(inside, 0.0, f[i])
            for p in reversed(range(GROUP)):
                value = value - along(f[i], j + p) * spread[p]
            f[i] = value
        for i in range(near, count):
            f[i] = jnp.where(inside, 0.0, f[i]) - update[8 * (i - near) : 8 * (i - near) + 8]
        for h in range(2):
            f[2 * g + h] = (rows[h] - lower[h] * swap(rows[h])) * jnp.sqrt(scale[h])
    return jnp.concatenate([jnp.where(lane <= sub + 8 * i, f[i], 0.0) for i in range(count)], axis=0)


def finish_kernel(regions, params, *refs):
    shapes = part_shapes(params)
    count = len(shapes)
    parts, refs = refs[:count], refs[count:]
    factor_ref, solved_ref = refs[:2]
    refs = refs[2:]
    alls, refs = refs[:count], refs[count:]
    recv1, refs = refs[:count], refs[count:]
    mine, refs = refs[:count], refs[count:]
    recv2, refs = refs[:count], refs[count:]
    a_ref, high_ref, low_ref, inv_high, inv_low, tile_ref, link_ref = refs[:7]
    s1, r1, s2, r2, s3, r3, s4, r4, s5, r5, s6, r6 = refs[7:]
    total = IMAGES * params
    own = params // 4
    half = params // 2
    stride = regions // CHUNKS
    region_at = lax.axis_index("region")
    row_at = lax.axis_index("row")
    col_at = lax.axis_index("col")
    chunk_at = region_at // stride
    owner = lax.rem(region_at, stride) == 0
    other = lax.rem(region_at, stride) != 0

    def device(region, row, col):
        return {"region": region, "row": row, "col": col}

    def remote(src, dst, send, recv, to):
        return pltpu.make_async_remote_copy(
            src_ref=src, dst_ref=dst, send_sem=send, recv_sem=recv, device_id=to, device_id_type=MESH
        )

    def landed(ref, recv):
        remote(ref, ref, s1.at[0], recv, partner).wait_recv()

    def guarded(when, action):
        if when is True:
            action()
        else:
            pl.when(when)(action)

    owns = True if stride == 1 else owner
    partner = device(region_at, 1 - row_at, col_at)
    along = [device(lax.rem(region_at + d, regions), row_at, col_at) for d in range(1, regions)]
    cols = [lax.rem(col_at + d, IMAGES) for d in range(IMAGES)]
    across = [device(region_at, row_at, c) for c in cols[1:]]
    others = [
        device(lax.rem(region_at + d, regions), row_at, cols[e])
        for d in range(regions)
        for e in range(IMAGES)
        if d + e > 0
    ]
    barrier = pltpu.get_barrier_semaphore()
    for peer in [partner] + others:
        pl.semaphore_signal(barrier, inc=1, device_id=peer, device_id_type=MESH)
    pl.semaphore_wait(barrier, 1 + len(others))
    sent = []

    def send(when, src, dst, sems, index, recv, to, like):
        sent.append((when, like, sems, index))
        guarded(when, lambda: remote(src, dst, sems.at[index], recv, to).start())

    def swap_cores(u):
        send(True, parts[u].at[1 - row_at], recv1[u], s1, (u,), r1.at[u], partner, lambda: recv1[u])

    def reduce_cores(u):
        landed(recv1[u], r1.at[u])
        mine[u][...] = (parts[u][row_at] + recv1[u][...]).astype(mine[u].dtype)
        for d in range(0 if stride > 1 else 1, CHUNKS):
            chunk = lax.rem(chunk_at + d, CHUNKS)
            to = chunk * stride
            gap = lax.rem(to - region_at + regions, regions)
            send(
                True if d else other,
                mine[u].at[chunk],
                recv2[u].at[gap - 1],
                s2,
                (u, d),
                r2.at[u, gap - 1],
                device(to, row_at, col_at),
                lambda: mine[u].at[0],
            )

    def reduce_regions(u):
        def add():
            value = mine[u][chunk_at].astype(jnp.float32)
            for gap in range(regions - 1):
                landed(recv2[u].at[gap], r2.at[u, gap])
                value = value + recv2[u][gap].astype(jnp.float32)
            alls[u][col_at, row_at, chunk_at] = value.astype(alls[u].dtype)

        guarded(owns, add)
        piece = alls[u].at[col_at, row_at, chunk_at]
        if u == 0:
            for i, peer in enumerate(others):
                send(owns, piece, piece, s6, (i,), r6.at[col_at, chunk_at], peer, lambda: mine[u].at[0])
        else:
            for d, peer in enumerate(along):
                send(owns, piece, piece, s3, (u, d,), r3.at[u, chunk_at], peer, lambda: mine[u].at[0])

    def forward(u, d):
        piece = alls[u].at[cols[d], row_at]
        send(True, piece, piece, s5, (u, d,), r5.at[u, cols[d]], partner, lambda: mine[u])

    def gather_regions(u):
        def arrive(e, d):
            chunk = lax.rem(chunk_at + d, CHUNKS)
            landed(alls[u].at[cols[e], row_at, chunk], r6.at[cols[e], chunk] if u == 0 else r3.at[u, chunk])

        for e in range(IMAGES if u == 0 else 1):
            for d in range(CHUNKS):
                if d + e > 0:
                    arrive(e, d)
                elif stride > 1:
                    guarded(other, lambda: arrive(0, 0))
            forward(u, e)
        if u > 0:
            piece = alls[u].at[col_at, row_at]
            for d, peer in enumerate(across):
                send(True, piece, piece, s4, (u, d,), r4.at[u, col_at], peer, lambda: mine[u])

    def gather_cols(u):
        for d in range(1, IMAGES):
            landed(alls[u].at[cols[d], row_at], r4.at[u, cols[d]])
            forward(u, d)

    def place(u):
        for d in range(IMAGES):
            landed(alls[u].at[cols[d], 1 - row_at], r5.at[u, cols[d]])
        b, diagonal = part_at(u)
        left = b * params
        for col in range(IMAGES):
            for core in range(2):
                for q in range(CHUNKS):
                    value = alls[u][col, core, q].astype(jnp.float32)
                    if diagonal:
                        row = b * params + col * own + (core * CHUNKS + q) * ROWS
                        a_ref[row : row + ROWS, left : left + params] += value
                    else:
                        wide = 2 * ROWS
                        at = left + q % 2 * half
                        for i in range(IMAGES - 1 - b):
                            row = (b + 1 + i) * params + col * own + (core * 2 + q // 2) * wide
                            a_ref[row : row + wide, at : at + half] += value[i * wide : (i + 1) * wide]
        if diagonal:
            for t in range(2):
                at = left + t * half
                a_ref[total : total + 1, at : at + half] += alls[u][0, 0, 0, t : t + 1, half:params]

    for u in range(count):
        swap_cores(u)
    a_ref[...] = jnp.zeros_like(a_ref)
    for u in range(4):
        reduce_cores(u)
    for u in range(4):
        reduce_regions(u)
    gather_regions(0)
    gather_regions(1)
    place(0)
    middle = {
        0: [(gather_regions, 2), (gather_regions, 3), (reduce_cores, 4), (reduce_cores, 5), (reduce_cores, 6)],
        1: [(gather_regions, 4), (gather_regions, 5), (gather_regions, 6)],
        2: [(gather_cols, 6)],
    }
    before = {
        0: [(gather_cols, 1), (gather_cols, 2), (place, 1)],
        1: [(place, 3)],
        2: [(place, 5)],
    }
    after = {
        0: [(gather_cols, 3), (reduce_regions, 4), (reduce_regions, 5), (reduce_regions, 6), (place, 2)],
        1: [(gather_cols, 4), (gather_cols, 5), (place, 4)],
        2: [(place, 6)],
    }
    eye_r = lax.broadcasted_iota(jnp.int32, (TILE, TILE), 0)
    eye_c = lax.broadcasted_iota(jnp.int32, (TILE, TILE), 1)
    damp = jnp.where(eye_r == eye_c, damping, 0.0).astype(jnp.float32)

    def panel(n, _):
        def at(t):
            return pl.ds(pl.multiple_of(n * params + t * TILE, TILE), TILE)

        def keep(t, e, value):
            high, low = split(value)
            inv_high[t * TILE : (t + 1) * TILE, e * TILE : (e + 1) * TILE] = high
            inv_low[t * TILE : (t + 1) * TILE, e * TILE : (e + 1) * TILE] = low

        first = a_ref[at(0), at(0)] + damp
        a_ref[at(0), at(0)] = first
        inv0 = eliminate(first)
        keep(0, 0, inv0)
        keep(0, 1, jnp.zeros((TILE, TILE), jnp.float32))
        split0 = split(inv0)
        below = split(product(split(a_ref[at(1), at(0)]), split0, NT))
        second = a_ref[at(1), at(1)] + damp
        a_ref[at(1), at(1)] = second
        tile_ref[...] = second - product(below, below, NT)
        link_ref[...] = product(below, split0, NN)
        for s in middle:

            @pl.when(n == s)
            def _():
                for action, u in middle[s]:
                    action(u)

        inv1 = eliminate(tile_ref[...])
        keep(1, 1, inv1)
        keep(1, 0, -product(split(inv1), split(link_ref[...]), NN))
        for s in range(IMAGES):

            @pl.when(n == s)
            def _():
                for action, u in before.get(s, []):
                    action(u)
                lo = s * params
                hi = lo + params
                end = total + EXTRA
                value = product(split(a_ref[lo:end, lo:hi]), (inv_high[...], inv_low[...]), NT)
                a_ref[lo:end, lo:hi] = value
                high, low = split(value)
                high_ref[lo:end, :] = high
                low_ref[lo:end, :] = low
                for c in range(s + 1, IMAGES):
                    col = slice(c * params, (c + 1) * params)
                    row = slice(c * params, end)
                    a_ref[row, col] -= product(
                        (high_ref[row, :], low_ref[row, :]), (high_ref[col, :], low_ref[col, :]), NT
                    )
                for action, u in after.get(s, []):
                    action(u)

        return 0

    lax.fori_loop(0, IMAGES, panel, 0)
    for when, like, sems, index in sent:
        guarded(when, lambda: remote(like(), like(), sems.at[index], r1.at[0], partner).wait_send())
    row_block = factor_ref.shape[0]
    first_row = pl.multiple_of((region_at * 2 + row_at) * row_block, row_block)
    first_col = pl.multiple_of(col_at * params, params)
    held = a_ref[pl.ds(first_row, row_block), pl.ds(first_col, params)]
    at_row = first_row + lax.broadcasted_iota(jnp.int32, held.shape, 0)
    at_col = first_col + lax.broadcasted_iota(jnp.int32, held.shape, 1)
    factor_ref[...] = jnp.where(at_row >= at_col, held, 0.0)
    solved_ref[...] = a_ref[total, :]


def emit_kernel(held_ref, whole_ref, factor_ref, solved_ref):
    factor_ref[...] = held_ref[...]
    solved_ref[...] = whole_ref[...]


def emit(held, whole):
    vmem = pl.BlockSpec(memory_space=pltpu.VMEM)
    return pl.pallas_call(
        emit_kernel,
        out_shape=(
            jax.ShapeDtypeStruct(held.shape, held.dtype),
            jax.ShapeDtypeStruct(whole.shape, whole.dtype),
        ),
        in_specs=[vmem, vmem],
        out_specs=(vmem, vmem),
        name="emit",
    )(held, whole)


def finish(parts, regions, params, row_block):
    shapes = part_shapes(params)
    count = len(shapes)
    types = [jnp.float32 if part_at(u)[1] else jnp.bfloat16 for u in range(count)]
    total = IMAGES * params
    dma = pltpu.SemaphoreType.DMA
    vmem = pl.BlockSpec(memory_space=pltpu.VMEM)
    peers = regions * IMAGES - 1
    return pl.pallas_call(
        functools.partial(finish_kernel, regions, params),
        out_shape=(
            jax.ShapeDtypeStruct((row_block, params), jnp.float32),
            jax.ShapeDtypeStruct((total,), jnp.float32),
        ),
        in_specs=[vmem] * count,
        out_specs=(vmem, vmem),
        scratch_shapes=[pltpu.VMEM((IMAGES,) + s, t) for s, t in zip(shapes, types)]
        + [pltpu.VMEM(s[1:], jnp.float32) for s in shapes]
        + [pltpu.VMEM(s[1:], t) for s, t in zip(shapes, types)]
        + [pltpu.VMEM((regions - 1,) + s[2:], t) for s, t in zip(shapes, types)]
        + [
            pltpu.VMEM((total + EXTRA, total), jnp.float32),
            pltpu.VMEM((total + EXTRA, params), jnp.bfloat16),
            pltpu.VMEM((total + EXTRA, params), jnp.bfloat16),
            pltpu.VMEM((params, params), jnp.bfloat16),
            pltpu.VMEM((params, params), jnp.bfloat16),
            pltpu.VMEM((TILE, TILE), jnp.float32),
            pltpu.VMEM((TILE, TILE), jnp.float32),
            dma((count,)),
            dma((count,)),
            dma((count, CHUNKS)),
            dma((count, regions - 1)),
            dma((count, regions - 1)),
            dma((count, CHUNKS)),
            dma((count, IMAGES - 1)),
            dma((count, IMAGES)),
            dma((count, IMAGES)),
            dma((count, IMAGES)),
            dma((peers,)),
            dma((IMAGES, CHUNKS)),
        ],
        compiler_params=pltpu.CompilerParams(
            collective_id=0, has_side_effects=True, vmem_limit_bytes=VMEM_LIMIT
        ),
        name="finish",
    )(*parts)


def on_device(cam_jac, point_rows, track_images, track_counts):
    regions = lax.axis_size("region")
    params = cam_jac.shape[2]
    row_block = IMAGES * params // (regions * lax.axis_size("row"))
    parts = accumulate(cam_jac, point_rows, track_images, track_counts)
    factor, solved = emit(*finish(parts, regions, params, row_block))
    return (factor, solved)


def solution(mesh):
    in_specs = (
        P(None, None, None, "region"),
        P(None, None, None, "region"),
        P(None, "region"),
        P(),
    )
    out_specs = (P(("region", "row"), "col"), P())
    return jax.shard_map(
        on_device, mesh=mesh, in_specs=in_specs, out_specs=out_specs, check_vma=False
    )
```

```python
import functools

import jax
import jax.numpy as jnp
from jax import lax
from jax.experimental import pallas as pl
from jax.experimental.pallas import tpu as pltpu
from jax.sharding import PartitionSpec as P

IMAGES = 4
CHUNKS = 4
ROWS = 8
BLOCK = 512
TILE = 128
EXTRA = 16
VMEM_LIMIT = 60 * 1024 * 1024

damping = 0.1
point_damping = 0.5

NT = (((1,), (1,)), ((), ()))
NN = (((1,), (0,)), ((), ()))
MESH = pl.DeviceIdType.MESH


def point_terms(pts):
    views = len(pts)
    pairs = [(k, r) for k in range(views) for r in range(2)]

    def entry(left, right):
        return sum(pts[k][r][left] * pts[k][r][right] for k, r in pairs)

    d1 = jnp.sqrt(entry(0, 0) + point_damping)
    b1 = entry(1, 0) / d1
    bf = entry(2, 0) / d1
    d2 = jnp.sqrt(entry(1, 1) + point_damping - b1 * b1)
    b2 = (entry(2, 1) - bf * b1) / d2
    d3 = jnp.sqrt(entry(2, 2) + point_damping - bf * bf - b2 * b2)

    def solve(first, second, third):
        o1 = first / d1
        o2 = (second - b1 * o1) / d2
        o3 = (third - bf * o1 - b2 * o2) / d3
        return [o.astype(jnp.bfloat16).astype(jnp.float32) for o in (o1, o2, o3)]

    coef = {(k, r): solve(*pts[k][r][0:3]) for k, r in pairs}
    step = solve(*[entry(c, 3) for c in range(3)])
    return coef, step


def part_at(u):
    return u // 2, u % 2 == 0


def part_shapes(params):
    shapes = []
    for u in range(2 * IMAGES - 1):
        b, diagonal = part_at(u)
        tail = (ROWS, params) if diagonal else ((IMAGES - 1 - b) * 2 * ROWS, params // 2)
        shapes.append((2, CHUNKS) + tail)
    return shapes


def accumulate_block(block, pos_ref, cam_ref, pts_ref, img_ref, accs, rhs, lhs):
    params=cam_ref.shape[2]
    views=cam_ref.shape[0]
    own=params//4
    step=pl.program_id(0)
    count=pos_ref[lax.axis_index("region")]
    row_at=lax.axis_index("row"); col_at=lax.axis_index("col")
    start=(2*step+row_at)*block
    sub=16
    @pl.when(step==0)
    def _():
        for a in accs: a[...]=jnp.zeros_like(a)
    slot=start+lax.broadcasted_iota(jnp.int32,(1,block),1)
    live=slot<count
    pts=[]
    for k in range(views):
        pts.append([])
        for r in range(2):
            wide=pts_ref[k,r].astype(jnp.float32)
            pts[k].append([wide[c:c+1,:] for c in range(4)])
    coef,y=point_terms(pts)
    images=[img_ref[k:k+1,:] for k in range(views)]
    zero=jnp.zeros((sub-2,block),jnp.float32)
    def pick(masks,values):
        out=jnp.zeros_like(values[0])
        for mask,value in zip(masks,values): out=jnp.where(mask,value,out)
        return out
    def widen(mask):
        return jnp.broadcast_to(mask.astype(jnp.float32),(sub,block)).astype(jnp.bfloat16)>0
    masks=[[(images[k]==a)&live for k in range(views)] for a in range(IMAGES)]
    wide=[[widen(m) for m in masks[a][:2]] for a in range(IMAGES)]
    c=[[[pick(masks[a],[coef[k,r][m] for k in range(views)]) for m in range(3)] for r in range(2)] for a in range(IMAGES)]
    held=[(masks[a][0]|masks[a][1]|masks[a][2]).astype(jnp.float32) for a in range(IMAGES)]
    err=[[pick(masks[a],[pts[k][r][3] for k in range(views)]) for r in range(2)] for a in range(IMAGES)]
    def chosen(a,at,r):
        j=[cam_ref[k,r,pl.ds(at,sub),:] for k in range(views)]
        return jnp.where(wide[a][0],j[0],jnp.where(wide[a][1],j[1],j[2]))
    mine=pl.multiple_of(col_at*own,own)
    for b in range(IMAGES):
        for i in range(params//sub):
            for r in range(2):
                rhs[b][i*sub:(i+1)*sub,r*block:(r+1)*block]=chosen(b,i*sub,r)
        for a in range(b,IMAGES):
            x={}
            for r in range(2):
                for s in range(2):
                    if a==b and s<r: x[r,s]=x[s,r]; continue
                    v=-(c[a][r][0]*c[b][s][0]+c[a][r][1]*c[b][s][1]+c[a][r][2]*c[b][s][2])
                    x[r,s]=v+held[a] if a==b and r==s else v
            for i in range(own//sub):
                jac=[chosen(a,mine+i*sub,r).astype(jnp.float32) for r in range(2)]
                for s in range(2):
                    v=jac[0]*x[0,s]+jac[1]*x[1,s]
                    lhs[b][(a-b)*own+i*sub:(a-b)*own+(i+1)*sub,s*block:(s+1)*block]=v.astype(jnp.bfloat16)
        depth=(IMAGES-b)*own
        for r in range(2):
            g=err[b][r]-(c[b][r][0]*y[0]+c[b][r][1]*y[1]+c[b][r][2]*y[2])
            near=g.astype(jnp.bfloat16).astype(jnp.float32)
            lhs[b][depth:depth+sub,r*block:(r+1)*block]=jnp.concatenate([near,g-near,zero],axis=0).astype(jnp.bfloat16)
        accs[b][...]+=lax.dot_general(lhs[b][...],rhs[b][...],NT,preferred_element_type=jnp.float32)


def split_parts(params, accs, outs):
    own = params // 4
    col_at = lax.axis_index("col")
    half=params//2
    for b in range(IMAGES):
        acc=accs[b]
        depth=(IMAGES-b)*own
        sub8=lax.broadcasted_iota(jnp.int32,(8,half),0)
        grad=acc[depth:depth+1,:]+acc[depth+1:depth+2,:]
        one=jnp.broadcast_to(grad[:,0:half],(8,half))
        two=jnp.broadcast_to(grad[:,half:params],(8,half))
        held=acc[0:8,half:params]
        grad=jnp.where(sub8==0,one,jnp.where(sub8==1,two,held))
        acc[0:8,half:params]=jnp.where(col_at==0,grad,held)
    for u, out in enumerate(outs):
        b, diagonal = part_at(u)
        acc = accs[b]
        for core in range(2):
            for q in range(CHUNKS):
                if diagonal:
                    src = (core * CHUNKS + q) * ROWS
                    out[core, q] = acc[src : src + ROWS, :]
                else:
                    wide = 2 * ROWS
                    at = q % 2 * half
                    for i in range(IMAGES - 1 - b):
                        src = (i + 1) * own + (core * 2 + q // 2) * wide
                        out[core, q, i * wide : (i + 1) * wide, :] = acc[src : src + wide, at : at + half]


def split(x):
    high = x.astype(jnp.bfloat16)
    return high, (x - high.astype(jnp.float32)).astype(jnp.bfloat16)


def product(left, right, dims):
    lh, ll = left
    rh, rl = right
    dot = functools.partial(lax.dot_general, dimension_numbers=dims, preferred_element_type=jnp.float32)
    return dot(lh, rh) + (dot(ll, rh) + dot(lh, rl))


def eliminate(tile):
    near = 2
    W=(8,TILE)
    sub=lax.broadcasted_iota(jnp.int32,W,0); lane=lax.broadcasted_iota(jnp.int32,W,1)
    other=sub+1-2*lax.rem(sub,2)
    zero=jnp.zeros(W,jnp.float32)
    V=TILE//8
    f=[tile[8*i:8*i+8,:] for i in range(V)]
    def swap(x): return jnp.take_along_axis(x,other,axis=0,mode="promise_in_bounds")
    def down(x,p): return jnp.broadcast_to(x[p:p+1,:],W)
    def along(x,l): return jnp.broadcast_to(x[:,l:l+1],W)
    def pivots(c,rest,R,RB):
        main=cross=lower=scale=zero
        for p in range(0,8,2):
            cp,cq=c[p],c[p+1]
            a,b,d=down(cp,p),down(cp,p+1),down(cq,p+1)
            det=a*d-b*b
            inv=1.0/det
            rp,rq=down(R,p),down(R,p+1)
            if p<6:
                keep=sub>p+1
                u=jnp.where(keep,d*cp-b*cq,0.0); v=jnp.where(keep,a*cq-b*cp,0.0)
                ui,vi=u*inv,v*inv
                for s in range(p+2,8):
                    cs,ct=down(cp,s),down(cq,s)
                    c[s]=c[s]-(u*cs+v*ct)*inv if s<p+4 else c[s]-ui*cs-vi*ct
                R=R-ui*rp-vi*rq
            if rest is not None:
                n,m=rest
                un,vn=d*n[p]-b*n[p+1],a*n[p+1]-b*n[p]
                uni,vni=un*inv,vn*inv
                for s in range(p+2,8): n[s]=n[s]-uni*down(cp,s)-vni*down(cq,s)
                for s in range(8):
                    ns,nt=down(n[p],s),down(n[p+1],s)
                    if p==6 and s<2: m[s]=m[s]-(un*ns+vn*nt)*inv
                    else: m[s]=m[s]-uni*ns-vni*nt
                RB=RB-uni*rp-vni*rq
            ia=1.0/a
            m0,m1=sub==p,sub==p+1
            main=jnp.where(m0,d*inv,jnp.where(m1,a*inv,main))
            cross=jnp.where(m0|m1,b*inv,cross)
            lower=jnp.where(m1,b*ia,lower)
            scale=jnp.where(m0,ia,jnp.where(m1,a*inv,scale))
        def pairs(x): return main*x-cross*swap(x)
        w=pairs(R)
        for q in (6,4,2):
            l0=jnp.where(sub<q,pairs(c[q]),0.0); l1=jnp.where(sub<q,pairs(c[q+1]),0.0)
            w=w-l0*down(w,q)-l1*down(w,q+1)
        out=(R-lower*swap(R))*jnp.sqrt(scale)
        return w,out,RB
    for g in range(V//2):
        j=16*g
        top,bot=f[2*g],f[2*g+1]
        in0=(lane>=j)&(lane<j+8); in1=(lane>=j+8)&(lane<j+16); both=in0|in1
        c=[along(top,j+s) for s in range(8)]
        n=[along(bot,j+s) for s in range(8)]
        m=[along(bot,j+8+s) for s in range(8)]
        R0=jnp.where(in0,(lane-j==sub).astype(jnp.float32),top)
        RB=jnp.where(in0,0.0,bot)
        w0,out0,RB=pivots(c,(n,m),R0,RB)
        R1=jnp.where(in1,(lane-j-8==sub).astype(jnp.float32),RB)
        lift=[along(w0,j+8+q) for q in range(8)]
        w1,out1,_=pivots(m,None,R1,None)
        w0=jnp.where(in1,0.0,w0)
        for q in reversed(range(8)): w0=w0-lift[q]*down(w1,q)
        w=[w0,w1]
        last=min(V,2*g+2+near)
        if last<V:
            wide=[zero]*V
            wide[2*g],wide[2*g+1]=w
            up=product(split(jnp.concatenate(f[last:],axis=0)),split(jnp.concatenate(wide,axis=0)),NN)
        spread=[down(w[p//8],p%8) for p in range(16)]
        for i in range(2*g+2,last):
            value=jnp.where(both,0.0,f[i])
            for p in reversed(range(16)): value=value-along(f[i],j+p)*spread[p]
            f[i]=value
        for i in range(last,V): f[i]=jnp.where(both,0.0,f[i])-up[8*(i-last):8*(i-last)+8]
        f[2*g],f[2*g+1]=out0,out1
    return jnp.concatenate([jnp.where(lane<=sub+8*i,f[i],0.0) for i in range(V)],axis=0)


def finish_kernel(regions, params, *refs):
    shapes = part_shapes(params)
    count = len(shapes)
    parts, refs = refs[:count], refs[count:]
    factor_ref, solved_ref = refs[:2]
    refs = refs[2:]
    alls, refs = refs[:count], refs[count:]
    recv1, refs = refs[:count], refs[count:]
    mine, refs = refs[:count], refs[count:]
    recv2, refs = refs[:count], refs[count:]
    a_ref, high_ref, low_ref, inv_high, inv_low, tile_ref, link_ref = refs[:7]
    s1, r1, s2, r2, s3, r3, s4, r4, s5, r5, s6, r6 = refs[7:]
    total = IMAGES * params
    own = params // 4
    half = params // 2
    stride = regions // CHUNKS
    region_at = lax.axis_index("region")
    row_at = lax.axis_index("row")
    col_at = lax.axis_index("col")
    chunk_at = region_at // stride
    owner = lax.rem(region_at, stride) == 0
    other = lax.rem(region_at, stride) != 0

    def device(region, row, col):
        return {"region": region, "row": row, "col": col}

    def remote(src, dst, send, recv, to):
        return pltpu.make_async_remote_copy(
            src_ref=src, dst_ref=dst, send_sem=send, recv_sem=recv, device_id=to, device_id_type=MESH
        )

    def landed(ref, recv):
        remote(ref, ref, s1.at[0], recv, partner).wait_recv()

    def guarded(when, action):
        if when is True:
            action()
        else:
            pl.when(when)(action)

    owns = True if stride == 1 else owner
    partner = device(region_at, 1 - row_at, col_at)
    along = [device(lax.rem(region_at + d, regions), row_at, col_at) for d in range(1, regions)]
    cols = [lax.rem(col_at + d, IMAGES) for d in range(IMAGES)]
    across = [device(region_at, row_at, c) for c in cols[1:]]
    others = [
        device(lax.rem(region_at + d, regions), row_at, cols[e])
        for d in range(regions)
        for e in range(IMAGES)
        if d + e > 0
    ]
    pl.semaphore_wait(pltpu.get_barrier_semaphore(), 1 + len(others))
    sent = []

    def send(when, src, dst, sems, index, recv, to, like):
        sent.append((when, like, sems, index))
        guarded(when, lambda: remote(src, dst, sems.at[index], recv, to).start())

    def swap_cores(u):
        send(True, parts[u].at[1 - row_at], recv1[u], s1, (u,), r1.at[u], partner, lambda: recv1[u])

    def reduce_cores(u):
        landed(recv1[u], r1.at[u])
        mine[u][...] = (parts[u][row_at] + recv1[u][...]).astype(mine[u].dtype)
        for d in range(0 if stride > 1 else 1, CHUNKS):
            chunk = lax.rem(chunk_at + d, CHUNKS)
            to = chunk * stride
            gap = lax.rem(to - region_at + regions, regions)
            send(
                True if d else other,
                mine[u].at[chunk],
                recv2[u].at[gap - 1],
                s2,
                (u, d),
                r2.at[u, gap - 1],
                device(to, row_at, col_at),
                lambda: mine[u].at[0],
            )

    def reduce_regions(u):
        def add():
            value = mine[u][chunk_at].astype(jnp.float32)
            for gap in range(regions - 1):
                landed(recv2[u].at[gap], r2.at[u, gap])
                value = value + recv2[u][gap].astype(jnp.float32)
            alls[u][col_at, row_at, chunk_at] = value.astype(alls[u].dtype)

        guarded(owns, add)
        piece = alls[u].at[col_at, row_at, chunk_at]
        if u == 0:
            for i, peer in enumerate(others):
                send(owns, piece, piece, s6, (i,), r6.at[col_at, chunk_at], peer, lambda: mine[u].at[0])
        else:
            for d, peer in enumerate(along):
                send(owns, piece, piece, s3, (u, d,), r3.at[u, chunk_at], peer, lambda: mine[u].at[0])

    def forward(u, d):
        piece = alls[u].at[cols[d], row_at]
        send(True, piece, piece, s5, (u, d,), r5.at[u, cols[d]], partner, lambda: mine[u])

    def gather_regions(u):
        def arrive(e, d):
            chunk = lax.rem(chunk_at + d, CHUNKS)
            landed(alls[u].at[cols[e], row_at, chunk], r6.at[cols[e], chunk] if u == 0 else r3.at[u, chunk])

        for e in range(IMAGES if u == 0 else 1):
            for d in range(CHUNKS):
                if d + e > 0:
                    arrive(e, d)
                elif stride > 1:
                    guarded(other, lambda: arrive(0, 0))
            forward(u, e)
        if u > 0:
            piece = alls[u].at[col_at, row_at]
            for d, peer in enumerate(across):
                send(True, piece, piece, s4, (u, d,), r4.at[u, col_at], peer, lambda: mine[u])

    def gather_cols(u):
        for d in range(1, IMAGES):
            landed(alls[u].at[cols[d], row_at], r4.at[u, cols[d]])
            forward(u, d)

    def place(u):
        for d in range(IMAGES):
            landed(alls[u].at[cols[d], 1 - row_at], r5.at[u, cols[d]])
        b, diagonal = part_at(u)
        left = b * params
        for col in range(IMAGES):
            for core in range(2):
                for q in range(CHUNKS):
                    value = alls[u][col, core, q].astype(jnp.float32)
                    if diagonal:
                        row = b * params + col * own + (core * CHUNKS + q) * ROWS
                        a_ref[row : row + ROWS, left : left + params] += value
                    else:
                        wide = 2 * ROWS
                        at = left + q % 2 * half
                        for i in range(IMAGES - 1 - b):
                            row = (b + 1 + i) * params + col * own + (core * 2 + q // 2) * wide
                            a_ref[row : row + wide, at : at + half] += value[i * wide : (i + 1) * wide]
        if diagonal:
            for t in range(2):
                at = left + t * half
                a_ref[total : total + 1, at : at + half] += alls[u][0, 0, 0, t : t + 1, half:params]

    for u in range(count):
        swap_cores(u)
    reduce_cores(0)
    reduce_cores(1)
    reduce_cores(2)
    reduce_cores(3)
    reduce_regions(0)
    reduce_regions(1)
    reduce_regions(2)
    reduce_regions(3)
    reduce_cores(4)
    reduce_cores(5)
    reduce_cores(6)
    gather_regions(0)
    gather_regions(1)
    place(0)
    middle = {
        0: [(gather_regions, 2), (gather_regions, 3), (reduce_regions, 4), (reduce_regions, 5), (reduce_regions, 6)],
        1: [],
        2: [],
    }
    before = {
        0: [(gather_cols, 1), (place, 1), (gather_cols, 2)],
        1: [(gather_cols, 4), (gather_cols, 5), (place, 3)],
        2: [(place, 5)],
    }
    after = {
        0: [(gather_cols, 3), (gather_regions, 4), (gather_regions, 5), (gather_regions, 6), (place, 2)],
        1: [(gather_cols, 6), (place, 4)],
        2: [(place, 6)],
    }
    eye_r = lax.broadcasted_iota(jnp.int32, (TILE, TILE), 0)
    eye_c = lax.broadcasted_iota(jnp.int32, (TILE, TILE), 1)
    damp = jnp.where(eye_r == eye_c, damping, 0.0).astype(jnp.float32)

    def panel(n, _):
        def at(t):
            return pl.ds(pl.multiple_of(n * params + t * TILE, TILE), TILE)

        def keep(t, e, value):
            high, low = split(value)
            inv_high[t * TILE : (t + 1) * TILE, e * TILE : (e + 1) * TILE] = high
            inv_low[t * TILE : (t + 1) * TILE, e * TILE : (e + 1) * TILE] = low

        first = a_ref[at(0), at(0)] + damp
        a_ref[at(0), at(0)] = first
        inv0 = eliminate(first)
        keep(0, 0, inv0)
        keep(0, 1, jnp.zeros((TILE, TILE), jnp.float32))
        split0 = split(inv0)
        below = split(product(split(a_ref[at(1), at(0)]), split0, NT))
        second = a_ref[at(1), at(1)] + damp
        a_ref[at(1), at(1)] = second
        tile_ref[...] = second - product(below, below, NT)
        link_ref[...] = product(below, split0, NN)
        for s in middle:

            @pl.when(n == s)
            def _():
                for action, u in middle[s]:
                    action(u)

        inv1 = eliminate(tile_ref[...])
        keep(1, 1, inv1)
        keep(1, 0, -product(split(inv1), split(link_ref[...]), NN))
        for s in range(IMAGES):

            @pl.when(n == s)
            def _():
                for action, u in before.get(s, []):
                    action(u)
                lo = s * params
                hi = lo + params
                end = total + EXTRA
                value = product(split(a_ref[lo:end, lo:hi]), (inv_high[...], inv_low[...]), NT)
                a_ref[lo:end, lo:hi] = value
                high, low = split(value)
                high_ref[lo:end, :] = high
                low_ref[lo:end, :] = low
                for c in range(s + 1, IMAGES):
                    col = slice(c * params, (c + 1) * params)
                    row = slice(c * params, end)
                    a_ref[row, col] -= product(
                        (high_ref[row, :], low_ref[row, :]), (high_ref[col, :], low_ref[col, :]), NT
                    )
                for action, u in after.get(s, []):
                    action(u)

        return 0

    lax.fori_loop(0, IMAGES, panel, 0)
    for when, like, sems, index in sent:
        guarded(when, lambda: remote(like(), like(), sems.at[index], r1.at[0], partner).wait_send())
    row_block = factor_ref.shape[0]
    first_row = pl.multiple_of((region_at * 2 + row_at) * row_block, row_block)
    first_col = pl.multiple_of(col_at * params, params)
    held = a_ref[pl.ds(first_row, row_block), pl.ds(first_col, params)]
    at_row = first_row + lax.broadcasted_iota(jnp.int32, held.shape, 0)
    at_col = first_col + lax.broadcasted_iota(jnp.int32, held.shape, 1)
    factor_ref[...] = jnp.where(at_row >= at_col, held, 0.0)
    solved_ref[...] = a_ref[total, :]


def greet(regions):
    region_at = lax.axis_index("region")
    row_at = lax.axis_index("row")
    col_at = lax.axis_index("col")
    barrier = pltpu.get_barrier_semaphore()
    pl.semaphore_signal(
        barrier,
        inc=1,
        device_id={"region": region_at, "row": 1 - row_at, "col": col_at},
        device_id_type=MESH,
    )
    for d in range(regions):
        for e in range(IMAGES):
            if d + e > 0:
                peer = {
                    "region": lax.rem(region_at + d, regions),
                    "row": row_at,
                    "col": lax.rem(col_at + e, IMAGES),
                }
                pl.semaphore_signal(barrier, inc=1, device_id=peer, device_id_type=MESH)


def step_kernel(regions, block, pos_ref, cam_ref, pts_ref, img_ref, factor_ref, solved_ref, *refs):
    params = cam_ref.shape[2]
    count = 2 * IMAGES - 1
    accs, rhs, lhs = refs[:IMAGES], refs[IMAGES : 2 * IMAGES], refs[2 * IMAGES : 3 * IMAGES]
    parts, refs = refs[3 * IMAGES : 3 * IMAGES + count], refs[3 * IMAGES + count :]

    @pl.when(pl.program_id(0) == 0)
    def _():
        greet(regions)
        refs[4 * count][...] = jnp.zeros_like(refs[4 * count])

    accumulate_block(block, pos_ref, cam_ref, pts_ref, img_ref, accs, rhs, lhs)

    @pl.when(pl.program_id(0) == pl.num_programs(0) - 1)
    def _():
        split_parts(params, accs, parts)
        finish_kernel(regions, params, *parts, factor_ref, solved_ref, *refs)


def run_steps(cam_jac, point_rows, track_images, track_counts, regions, row_block):
    views, _, params, slots = cam_jac.shape
    block = min(BLOCK, slots // 2)
    own = params // 4
    shapes = part_shapes(params)
    count = len(shapes)
    types = [jnp.float32 if part_at(u)[1] else jnp.bfloat16 for u in range(count)]
    total = IMAGES * params
    dma = pltpu.SemaphoreType.DMA
    peers = regions * IMAGES - 1
    depths = [(IMAGES - b) * own + 16 for b in range(IMAGES)]

    def at(i):
        return 2 * i + lax.axis_index("row")

    return pl.pallas_call(
        functools.partial(step_kernel, regions, block),
        out_shape=(
            jax.ShapeDtypeStruct((row_block, params), jnp.float32),
            jax.ShapeDtypeStruct((total,), jnp.float32),
        ),
        grid=(slots // block // 2,),
        in_specs=[
            pl.BlockSpec(memory_space=pltpu.SMEM),
            pl.BlockSpec((views, 2, params, block), lambda i: (0, 0, 0, at(i))),
            pl.BlockSpec((views, 2, 4, block), lambda i: (0, 0, 0, at(i))),
            pl.BlockSpec((views, block), lambda i: (0, at(i))),
        ],
        out_specs=(
            pl.BlockSpec((row_block, params), lambda i: (0, 0)),
            pl.BlockSpec((total,), lambda i: (0,)),
        ),
        scratch_shapes=[pltpu.VMEM((d, params), jnp.float32) for d in depths]
        + [pltpu.VMEM((params, 2 * block), jnp.bfloat16) for d in depths]
        + [pltpu.VMEM((d, 2 * block), jnp.bfloat16) for d in depths]
        + [pltpu.VMEM(s, jnp.float32) for s in shapes]
        + [pltpu.VMEM((IMAGES,) + s, t) for s, t in zip(shapes, types)]
        + [pltpu.VMEM(s[1:], jnp.float32) for s in shapes]
        + [pltpu.VMEM(s[1:], t) for s, t in zip(shapes, types)]
        + [pltpu.VMEM((regions - 1,) + s[2:], t) for s, t in zip(shapes, types)]
        + [
            pltpu.VMEM((total + EXTRA, total), jnp.float32),
            pltpu.VMEM((total + EXTRA, params), jnp.bfloat16),
            pltpu.VMEM((total + EXTRA, params), jnp.bfloat16),
            pltpu.VMEM((params, params), jnp.bfloat16),
            pltpu.VMEM((params, params), jnp.bfloat16),
            pltpu.VMEM((TILE, TILE), jnp.float32),
            pltpu.VMEM((TILE, TILE), jnp.float32),
            dma((count,)),
            dma((count,)),
            dma((count, CHUNKS)),
            dma((count, regions - 1)),
            dma((count, regions - 1)),
            dma((count, CHUNKS)),
            dma((count, IMAGES - 1)),
            dma((count, IMAGES)),
            dma((count, IMAGES)),
            dma((count, IMAGES)),
            dma((peers,)),
            dma((IMAGES, CHUNKS)),
        ],
        compiler_params=pltpu.CompilerParams(
            collective_id=0,
            has_side_effects=True,
            vmem_limit_bytes=VMEM_LIMIT,
            dimension_semantics=("arbitrary",),
        ),
        name="reduce_and_factor",
    )(track_counts, cam_jac, point_rows, track_images)


def emit_kernel(held_ref, whole_ref, factor_ref, solved_ref):
    factor_ref[...] = held_ref[...]
    solved_ref[...] = whole_ref[...]


def emit(held, whole):
    vmem = pl.BlockSpec(memory_space=pltpu.VMEM)
    return pl.pallas_call(
        emit_kernel,
        out_shape=(
            jax.ShapeDtypeStruct(held.shape, held.dtype),
            jax.ShapeDtypeStruct(whole.shape, whole.dtype),
        ),
        in_specs=[vmem, vmem],
        out_specs=(vmem, vmem),
        name="emit",
    )(held, whole)


def on_device(cam_jac, point_rows, track_images, track_counts):
    regions = lax.axis_size("region")
    params = cam_jac.shape[2]
    row_block = IMAGES * params // (regions * lax.axis_size("row"))
    factor, solved = emit(
        *run_steps(cam_jac, point_rows, track_images, track_counts, regions, row_block)
    )
    return (factor, solved)


def solution(mesh):
    in_specs = (
        P(None, None, None, "region"),
        P(None, None, None, "region"),
        P(None, "region"),
        P(),
    )
    out_specs = (P(("region", "row"), "col"), P())
    return jax.shard_map(
        on_device, mesh=mesh, in_specs=in_specs, out_specs=out_specs, check_vma=False
    )
```

```python
import functools

import jax
import jax.numpy as jnp
from jax import lax
from jax.experimental import pallas as pl
from jax.experimental.pallas import tpu as pltpu
from jax.sharding import PartitionSpec as P

IMAGES = 4
CHUNKS = 4
ROWS = 8
BLOCK = 512
TILE = 128
EXTRA = 16
VMEM_LIMIT = 60 * 1024 * 1024

damping = 0.1
point_damping = 0.5

NT = (((1,), (1,)), ((), ()))
NN = (((1,), (0,)), ((), ()))
MESH = pl.DeviceIdType.MESH


def point_terms(pts):
    views = len(pts)
    pairs = [(k, r) for k in range(views) for r in range(2)]

    def entry(left, right):
        return sum(pts[k][r][left] * pts[k][r][right] for k, r in pairs)

    d1 = jnp.sqrt(entry(0, 0) + point_damping)
    b1 = entry(1, 0) / d1
    bf = entry(2, 0) / d1
    d2 = jnp.sqrt(entry(1, 1) + point_damping - b1 * b1)
    b2 = (entry(2, 1) - bf * b1) / d2
    d3 = jnp.sqrt(entry(2, 2) + point_damping - bf * bf - b2 * b2)

    def solve(first, second, third):
        o1 = first / d1
        o2 = (second - b1 * o1) / d2
        o3 = (third - bf * o1 - b2 * o2) / d3
        return [o.astype(jnp.bfloat16).astype(jnp.float32) for o in (o1, o2, o3)]

    coef = {(k, r): solve(*pts[k][r][0:3]) for k, r in pairs}
    step = solve(*[entry(c, 3) for c in range(3)])
    return coef, step


def part_at(u):
    return u // 2, u % 2 == 0


def part_shapes(params):
    shapes = []
    for u in range(2 * IMAGES - 1):
        b, diagonal = part_at(u)
        tail = (ROWS, params) if diagonal else ((IMAGES - 1 - b) * 2 * ROWS, params // 2)
        shapes.append((2, CHUNKS) + tail)
    return shapes


def accumulate_block(block, turn, images_at, pos_ref, cam_ref, pts_ref, img_ref, accs, rhs, lhs):
    params=cam_ref.shape[2]
    views=cam_ref.shape[0]
    own=params//4
    count=pos_ref[lax.axis_index("region")]
    row_at=lax.axis_index("row"); col_at=lax.axis_index("col")
    start=(2*turn+row_at)*block
    sub=16
    slot=start+lax.broadcasted_iota(jnp.int32,(1,block),1)
    live=slot<count
    pts=[]
    for k in range(views):
        pts.append([])
        for r in range(2):
            wide=pts_ref[k,r].astype(jnp.float32)
            pts[k].append([wide[c:c+1,:] for c in range(4)])
    coef,y=point_terms(pts)
    images=[img_ref[k:k+1,:] for k in range(views)]
    zero=jnp.zeros((sub-2,block),jnp.float32)
    def pick(masks,values):
        out=jnp.zeros_like(values[0])
        for mask,value in zip(masks,values): out=jnp.where(mask,value,out)
        return out
    def widen(mask):
        return jnp.broadcast_to(mask.astype(jnp.float32),(sub,block)).astype(jnp.bfloat16)>0
    masks=[[(images[k]==a)&live for k in range(views)] for a in range(IMAGES)]
    wide=[[widen(m) for m in masks[a][:2]] for a in range(IMAGES)]
    c=[[[pick(masks[a],[coef[k,r][m] for k in range(views)]) for m in range(3)] for r in range(2)] for a in range(IMAGES)]
    held=[(masks[a][0]|masks[a][1]|masks[a][2]).astype(jnp.float32) for a in range(IMAGES)]
    err=[[pick(masks[a],[pts[k][r][3] for k in range(views)]) for r in range(2)] for a in range(IMAGES)]
    def chosen(a,at,r):
        j=[cam_ref[k,r,pl.ds(at,sub),:] for k in range(views)]
        return jnp.where(wide[a][0],j[0],jnp.where(wide[a][1],j[1],j[2]))
    mine=pl.multiple_of(col_at*own,own)
    for b in images_at:
        for i in range(params//sub):
            for r in range(2):
                rhs[b][i*sub:(i+1)*sub,r*block:(r+1)*block]=chosen(b,i*sub,r)
        for a in range(b,IMAGES):
            x={}
            for r in range(2):
                for s in range(2):
                    if a==b and s<r: x[r,s]=x[s,r]; continue
                    v=-(c[a][r][0]*c[b][s][0]+c[a][r][1]*c[b][s][1]+c[a][r][2]*c[b][s][2])
                    x[r,s]=v+held[a] if a==b and r==s else v
            for i in range(own//sub):
                jac=[chosen(a,mine+i*sub,r).astype(jnp.float32) for r in range(2)]
                for s in range(2):
                    v=jac[0]*x[0,s]+jac[1]*x[1,s]
                    lhs[b][(a-b)*own+i*sub:(a-b)*own+(i+1)*sub,s*block:(s+1)*block]=v.astype(jnp.bfloat16)
        depth=(IMAGES-b)*own
        for r in range(2):
            g=err[b][r]-(c[b][r][0]*y[0]+c[b][r][1]*y[1]+c[b][r][2]*y[2])
            near=g.astype(jnp.bfloat16).astype(jnp.float32)
            lhs[b][depth:depth+sub,r*block:(r+1)*block]=jnp.concatenate([near,g-near,zero],axis=0).astype(jnp.bfloat16)
        accs[b][...]+=lax.dot_general(lhs[b][...],rhs[b][...],NT,preferred_element_type=jnp.float32)


def split_parts(params, images_at, accs, outs):
    own = params // 4
    col_at = lax.axis_index("col")
    half=params//2
    for b in images_at:
        acc=accs[b]
        depth=(IMAGES-b)*own
        sub8=lax.broadcasted_iota(jnp.int32,(8,half),0)
        grad=acc[depth:depth+1,:]+acc[depth+1:depth+2,:]
        one=jnp.broadcast_to(grad[:,0:half],(8,half))
        two=jnp.broadcast_to(grad[:,half:params],(8,half))
        held=acc[0:8,half:params]
        grad=jnp.where(sub8==0,one,jnp.where(sub8==1,two,held))
        acc[0:8,half:params]=jnp.where(col_at==0,grad,held)
    for u, out in enumerate(outs):
        b, diagonal = part_at(u)
        if b not in images_at:
            continue
        acc = accs[b]
        for core in range(2):
            for q in range(CHUNKS):
                if diagonal:
                    src = (core * CHUNKS + q) * ROWS
                    out[core, q] = acc[src : src + ROWS, :]
                else:
                    wide = 2 * ROWS
                    at = q % 2 * half
                    for i in range(IMAGES - 1 - b):
                        src = (i + 1) * own + (core * 2 + q // 2) * wide
                        out[core, q, i * wide : (i + 1) * wide, :] = acc[src : src + wide, at : at + half]


def split(x):
    high = x.astype(jnp.bfloat16)
    return high, (x - high.astype(jnp.float32)).astype(jnp.bfloat16)


def product(left, right, dims):
    lh, ll = left
    rh, rl = right
    (lc, rc), _ = dims
    return lax.dot_general(
        jnp.concatenate([lh, ll, lh], axis=lc[0]),
        jnp.concatenate([rh, rh, rl], axis=rc[0]),
        dims,
        preferred_element_type=jnp.float32,
    )


def product_parts(left, right, dims):
    lh, ll = left
    rh, rl = right
    dot = functools.partial(lax.dot_general, dimension_numbers=dims, preferred_element_type=jnp.float32)
    return dot(lh, rh) + (dot(ll, rh) + dot(lh, rl))


def eliminate(tile):
    near = 2
    W=(8,TILE)
    sub=lax.broadcasted_iota(jnp.int32,W,0); lane=lax.broadcasted_iota(jnp.int32,W,1)
    other=sub+1-2*lax.rem(sub,2)
    zero=jnp.zeros(W,jnp.float32)
    V=TILE//8
    f=[tile[8*i:8*i+8,:] for i in range(V)]
    def swap(x): return jnp.take_along_axis(x,other,axis=0,mode="promise_in_bounds")
    def down(x,p): return jnp.broadcast_to(x[p:p+1,:],W)
    def along(x,l): return jnp.broadcast_to(x[:,l:l+1],W)
    def pivots(c,rest,R,RB):
        main=cross=lower=scale=zero
        for p in range(0,8,2):
            cp,cq=c[p],c[p+1]
            a,b,d=down(cp,p),down(cp,p+1),down(cq,p+1)
            det=a*d-b*b
            inv=1.0/det
            rp,rq=down(R,p),down(R,p+1)
            if p<6:
                keep=sub>p+1
                u=jnp.where(keep,d*cp-b*cq,0.0); v=jnp.where(keep,a*cq-b*cp,0.0)
                ui,vi=u*inv,v*inv
                for s in range(p+2,8):
                    cs,ct=down(cp,s),down(cq,s)
                    c[s]=c[s]-(u*cs+v*ct)*inv if s<p+4 else c[s]-ui*cs-vi*ct
                R=R-ui*rp-vi*rq
            if rest is not None:
                n,m=rest
                un,vn=d*n[p]-b*n[p+1],a*n[p+1]-b*n[p]
                uni,vni=un*inv,vn*inv
                for s in range(p+2,8): n[s]=n[s]-uni*down(cp,s)-vni*down(cq,s)
                for s in range(8):
                    ns,nt=down(n[p],s),down(n[p+1],s)
                    if p==6 and s<2: m[s]=m[s]-(un*ns+vn*nt)*inv
                    else: m[s]=m[s]-uni*ns-vni*nt
                RB=RB-uni*rp-vni*rq
            ia=1.0/a
            m0,m1=sub==p,sub==p+1
            main=jnp.where(m0,d*inv,jnp.where(m1,a*inv,main))
            cross=jnp.where(m0|m1,b*inv,cross)
            lower=jnp.where(m1,b*ia,lower)
            scale=jnp.where(m0,ia,jnp.where(m1,a*inv,scale))
        def pairs(x): return main*x-cross*swap(x)
        w=pairs(R)
        for q in (6,4,2):
            l0=jnp.where(sub<q,pairs(c[q]),0.0); l1=jnp.where(sub<q,pairs(c[q+1]),0.0)
            w=w-l0*down(w,q)-l1*down(w,q+1)
        out=(R-lower*swap(R))*jnp.sqrt(scale)
        return w,out,RB
    for g in range(V//2):
        j=16*g
        top,bot=f[2*g],f[2*g+1]
        in0=(lane>=j)&(lane<j+8); in1=(lane>=j+8)&(lane<j+16); both=in0|in1
        c=[along(top,j+s) for s in range(8)]
        n=[along(bot,j+s) for s in range(8)]
        m=[along(bot,j+8+s) for s in range(8)]
        R0=jnp.where(in0,(lane-j==sub).astype(jnp.float32),top)
        RB=jnp.where(in0,0.0,bot)
        w0,out0,RB=pivots(c,(n,m),R0,RB)
        R1=jnp.where(in1,(lane-j-8==sub).astype(jnp.float32),RB)
        lift=[along(w0,j+8+q) for q in range(8)]
        w1,out1,_=pivots(m,None,R1,None)
        w0=jnp.where(in1,0.0,w0)
        for q in reversed(range(8)): w0=w0-lift[q]*down(w1,q)
        w=[w0,w1]
        last=min(V,2*g+2+near)
        if last<V:
            wide=[zero]*V
            wide[2*g],wide[2*g+1]=w
            up=product_parts(split(jnp.concatenate(f[last:],axis=0)),split(jnp.concatenate(wide,axis=0)),NN)
        spread=[down(w[p//8],p%8) for p in range(16)]
        for i in range(2*g+2,last):
            value=jnp.where(both,0.0,f[i])
            for p in reversed(range(16)): value=value-along(f[i],j+p)*spread[p]
            f[i]=value
        for i in range(last,V): f[i]=jnp.where(both,0.0,f[i])-up[8*(i-last):8*(i-last)+8]
        f[2*g],f[2*g+1]=out0,out1
    return jnp.concatenate([jnp.where(lane<=sub+8*i,f[i],0.0) for i in range(V)],axis=0)


def finish_kernel(regions, params, turns, work, divide, *refs):
    shapes = part_shapes(params)
    count = len(shapes)
    parts, refs = refs[:count], refs[count:]
    factor_ref, solved_ref = refs[:2]
    refs = refs[2:]
    alls, refs = refs[:count], refs[count:]
    recv1, refs = refs[:count], refs[count:]
    mine, refs = refs[:count], refs[count:]
    recv2, refs = refs[:count], refs[count:]
    a_ref, high_ref, low_ref, inv_high, inv_low, tile_ref, link_ref = refs[:7]
    s1, r1, s2, r2, s3, r3, s4, r4, s5, r5, s6, r6 = refs[7:]
    total = IMAGES * params
    own = params // 4
    half = params // 2
    stride = regions // CHUNKS
    region_at = lax.axis_index("region")
    row_at = lax.axis_index("row")
    col_at = lax.axis_index("col")
    chunk_at = region_at // stride
    owner = lax.rem(region_at, stride) == 0
    other = lax.rem(region_at, stride) != 0

    def device(region, row, col):
        return {"region": region, "row": row, "col": col}

    def remote(src, dst, send, recv, to):
        return pltpu.make_async_remote_copy(
            src_ref=src, dst_ref=dst, send_sem=send, recv_sem=recv, device_id=to, device_id_type=MESH
        )

    def landed(ref, recv):
        remote(ref, ref, s1.at[0], recv, partner).wait_recv()

    def guarded(when, action):
        if when is True:
            action()
        else:
            pl.when(when)(action)

    owns = True if stride == 1 else owner
    partner = device(region_at, 1 - row_at, col_at)
    along = [device(lax.rem(region_at + d, regions), row_at, col_at) for d in range(1, regions)]
    cols = [lax.rem(col_at + d, IMAGES) for d in range(IMAGES)]
    across = [device(region_at, row_at, c) for c in cols[1:]]
    others = [
        device(lax.rem(region_at + d, regions), row_at, cols[e])
        for d in range(regions)
        for e in range(IMAGES)
        if d + e > 0
    ]
    sent = []

    def send(when, src, dst, sems, index, recv, to, like):
        sent.append((when, like, sems, index))
        guarded(when, lambda: remote(src, dst, sems.at[index], recv, to).start())

    def swap_cores(u):
        send(True, parts[u].at[1 - row_at], recv1[u], s1, (u,), r1.at[u], partner, lambda: recv1[u])

    def reduce_cores(u):
        landed(recv1[u], r1.at[u])
        mine[u][...] = (parts[u][row_at] + recv1[u][...]).astype(mine[u].dtype)
        for d in range(0 if stride > 1 else 1, CHUNKS):
            chunk = lax.rem(chunk_at + d, CHUNKS)
            to = chunk * stride
            gap = lax.rem(to - region_at + regions, regions)
            send(
                True if d else other,
                mine[u].at[chunk],
                recv2[u].at[gap - 1],
                s2,
                (u, d),
                r2.at[u, gap - 1],
                device(to, row_at, col_at),
                lambda: mine[u].at[0],
            )

    def reduce_regions(u):
        def add():
            value = mine[u][chunk_at].astype(jnp.float32)
            for gap in range(regions - 1):
                landed(recv2[u].at[gap], r2.at[u, gap])
                value = value + recv2[u][gap].astype(jnp.float32)
            alls[u][col_at, row_at, chunk_at] = value.astype(alls[u].dtype)

        guarded(owns, add)
        piece = alls[u].at[col_at, row_at, chunk_at]
        if u == 0:
            for i, peer in enumerate(others):
                send(owns, piece, piece, s6, (i,), r6.at[col_at, chunk_at], peer, lambda: mine[u].at[0])
        else:
            for d, peer in enumerate(along):
                send(owns, piece, piece, s3, (u, d,), r3.at[u, chunk_at], peer, lambda: mine[u].at[0])

    def forward(u, d):
        piece = alls[u].at[cols[d], row_at]
        send(True, piece, piece, s5, (u, d,), r5.at[u, cols[d]], partner, lambda: mine[u])

    def gather_regions(u):
        def arrive(e, d):
            chunk = lax.rem(chunk_at + d, CHUNKS)
            landed(alls[u].at[cols[e], row_at, chunk], r6.at[cols[e], chunk] if u == 0 else r3.at[u, chunk])

        for e in range(IMAGES if u == 0 else 1):
            for d in range(CHUNKS):
                if d + e > 0:
                    arrive(e, d)
                elif stride > 1:
                    guarded(other, lambda: arrive(0, 0))
            forward(u, e)
        if u > 0:
            piece = alls[u].at[col_at, row_at]
            for d, peer in enumerate(across):
                send(True, piece, piece, s4, (u, d,), r4.at[u, col_at], peer, lambda: mine[u])

    def gather_cols(u):
        for d in range(1, IMAGES):
            landed(alls[u].at[cols[d], row_at], r4.at[u, cols[d]])
            forward(u, d)

    def place(u):
        for d in range(IMAGES):
            landed(alls[u].at[cols[d], 1 - row_at], r5.at[u, cols[d]])
        b, diagonal = part_at(u)
        left = b * params
        for col in range(IMAGES):
            for core in range(2):
                for q in range(CHUNKS):
                    value = alls[u][col, core, q].astype(jnp.float32)
                    if diagonal:
                        row = b * params + col * own + (core * CHUNKS + q) * ROWS
                        a_ref[row : row + ROWS, left : left + params] += value
                    else:
                        wide = 2 * ROWS
                        at = left + q % 2 * half
                        for i in range(IMAGES - 1 - b):
                            row = (b + 1 + i) * params + col * own + (core * 2 + q // 2) * wide
                            a_ref[row : row + wide, at : at + half] += value[i * wide : (i + 1) * wide]
        if diagonal:
            for t in range(2):
                at = left + t * half
                a_ref[total : total + 1, at : at + half] += alls[u][0, 0, 0, t : t + 1, half:params]

    step = pl.program_id(0)
    last = turns - 1
    phases = [[0, 1], [2, 3]]
    marks = {
        last: [(swap_cores, u) for u in range(4)],
        turns: [(reduce_cores, 0), (reduce_cores, 1)],
        turns + 1: [(reduce_cores, 2), (reduce_cores, 3)],
        turns + last: [(reduce_regions, 0), (reduce_regions, 1), (swap_cores, 4), (swap_cores, 5), (swap_cores, 6)],
    }
    for phase, images_at in enumerate(phases):

        @pl.when(step // turns == phase)
        def _():
            work(lax.rem(step, turns), images_at)

        for turn in range(turns):
            mark = phase * turns + turn
            if turn < last and mark not in marks:
                continue

            @pl.when(step == mark)
            def _():
                if turn == last:
                    divide(images_at)
                if mark == last:
                    pl.semaphore_wait(pltpu.get_barrier_semaphore(), 1 + len(others))
                for action, u in marks[mark]:
                    action(u)

    def finish():
        for u in range(4, count):
            reduce_cores(u)
        reduce_regions(2)
        reduce_regions(3)
        gather_regions(0)
        gather_regions(1)
        place(0)
        middle = {
            0: [(gather_regions, 2), (gather_regions, 3), (reduce_regions, 4), (reduce_regions, 5), (reduce_regions, 6)],
            1: [],
            2: [],
        }
        before = {
            0: [(gather_cols, 1), (place, 1), (gather_cols, 2)],
            1: [(gather_cols, 4), (gather_cols, 5), (place, 3)],
            2: [(place, 5)],
        }
        after = {
            0: [(gather_cols, 3), (gather_regions, 4), (gather_regions, 5), (gather_regions, 6), (place, 2)],
            1: [(gather_cols, 6), (place, 4)],
            2: [(place, 6)],
        }
        eye_r = lax.broadcasted_iota(jnp.int32, (TILE, TILE), 0)
        eye_c = lax.broadcasted_iota(jnp.int32, (TILE, TILE), 1)
        damp = jnp.where(eye_r == eye_c, damping, 0.0).astype(jnp.float32)

        def panel(n, _):
            def at(t):
                return pl.ds(pl.multiple_of(n * params + t * TILE, TILE), TILE)

            def keep(t, e, value):
                high, low = split(value)
                inv_high[t * TILE : (t + 1) * TILE, e * TILE : (e + 1) * TILE] = high
                inv_low[t * TILE : (t + 1) * TILE, e * TILE : (e + 1) * TILE] = low

            first = a_ref[at(0), at(0)] + damp
            a_ref[at(0), at(0)] = first
            inv0 = eliminate(first)
            keep(0, 0, inv0)
            keep(0, 1, jnp.zeros((TILE, TILE), jnp.float32))
            split0 = split(inv0)
            below = split(product(split(a_ref[at(1), at(0)]), split0, NT))
            second = a_ref[at(1), at(1)] + damp
            a_ref[at(1), at(1)] = second
            tile_ref[...] = second - product(below, below, NT)
            link_ref[...] = product(below, split0, NN)
            for s in middle:

                @pl.when(n == s)
                def _():
                    for action, u in middle[s]:
                        action(u)

            inv1 = eliminate(tile_ref[...])
            keep(1, 1, inv1)
            keep(1, 0, -product(split(inv1), split(link_ref[...]), NN))
            for s in range(IMAGES):

                @pl.when(n == s)
                def _():
                    for action, u in before.get(s, []):
                        action(u)
                    lo = s * params
                    hi = lo + params
                    end = total + EXTRA
                    value = product(split(a_ref[lo:end, lo:hi]), (inv_high[...], inv_low[...]), NT)
                    a_ref[lo:end, lo:hi] = value
                    high, low = split(value)
                    high_ref[lo:end, :] = high
                    low_ref[lo:end, :] = low
                    for c in range(s + 1, IMAGES):
                        col = slice(c * params, (c + 1) * params)
                        row = slice(c * params, end)
                        a_ref[row, col] -= product(
                            (high_ref[row, :], low_ref[row, :]), (high_ref[col, :], low_ref[col, :]), NT
                        )
                    for action, u in after.get(s, []):
                        action(u)

            return 0

        lax.fori_loop(0, IMAGES, panel, 0)
        for when, like, sems, index in sent:
            guarded(when, lambda: remote(like(), like(), sems.at[index], r1.at[0], partner).wait_send())
        row_block = factor_ref.shape[0]
        first_row = pl.multiple_of((region_at * 2 + row_at) * row_block, row_block)
        first_col = pl.multiple_of(col_at * params, params)
        held = a_ref[pl.ds(first_row, row_block), pl.ds(first_col, params)]
        at_row = first_row + lax.broadcasted_iota(jnp.int32, held.shape, 0)
        at_col = first_col + lax.broadcasted_iota(jnp.int32, held.shape, 1)
        factor_ref[...] = jnp.where(at_row >= at_col, held, 0.0)
        solved_ref[...] = a_ref[total, :]

    pl.when(step == pl.num_programs(0) - 1)(finish)


def greet(regions):
    region_at = lax.axis_index("region")
    row_at = lax.axis_index("row")
    col_at = lax.axis_index("col")
    barrier = pltpu.get_barrier_semaphore()
    pl.semaphore_signal(
        barrier,
        inc=1,
        device_id={"region": region_at, "row": 1 - row_at, "col": col_at},
        device_id_type=MESH,
    )
    for d in range(regions):
        for e in range(IMAGES):
            if d + e > 0:
                peer = {
                    "region": lax.rem(region_at + d, regions),
                    "row": row_at,
                    "col": lax.rem(col_at + e, IMAGES),
                }
                pl.semaphore_signal(barrier, inc=1, device_id=peer, device_id_type=MESH)


def step_kernel(regions, block, turns, pos_ref, cam_ref, pts_ref, img_ref, factor_ref, solved_ref, *refs):
    params = cam_ref.shape[2]
    count = 2 * IMAGES - 1
    accs, rhs, lhs = refs[:IMAGES], refs[IMAGES : 2 * IMAGES], refs[2 * IMAGES : 3 * IMAGES]
    parts, refs = refs[3 * IMAGES : 3 * IMAGES + count], refs[3 * IMAGES + count :]

    @pl.when(pl.program_id(0) == 0)
    def _():
        greet(regions)
        refs[4 * count][...] = jnp.zeros_like(refs[4 * count])
        for acc in accs:
            acc[...] = jnp.zeros_like(acc)

    def work(turn, images_at):
        accumulate_block(block, turn, images_at, pos_ref, cam_ref, pts_ref, img_ref, accs, rhs, lhs)

    def divide(images_at):
        split_parts(params, images_at, accs, parts)

    finish_kernel(regions, params, turns, work, divide, *parts, factor_ref, solved_ref, *refs)


def run_steps(cam_jac, point_rows, track_images, track_counts, regions, row_block):
    views, _, params, slots = cam_jac.shape
    block = min(BLOCK, slots // 2)
    turns = slots // block // 2
    own = params // 4
    shapes = part_shapes(params)
    count = len(shapes)
    types = [jnp.float32 if part_at(u)[1] else jnp.bfloat16 for u in range(count)]
    total = IMAGES * params
    dma = pltpu.SemaphoreType.DMA
    peers = regions * IMAGES - 1
    depths = [(IMAGES - b) * own + 16 for b in range(IMAGES)]

    def at(i):
        return 2 * lax.rem(i, turns) + lax.axis_index("row")

    return pl.pallas_call(
        functools.partial(step_kernel, regions, block, turns),
        out_shape=(
            jax.ShapeDtypeStruct((row_block, params), jnp.float32),
            jax.ShapeDtypeStruct((total,), jnp.float32),
        ),
        grid=(2 * turns,),
        in_specs=[
            pl.BlockSpec(memory_space=pltpu.SMEM),
            pl.BlockSpec((views, 2, params, block), lambda i: (0, 0, 0, at(i))),
            pl.BlockSpec((views, 2, 4, block), lambda i: (0, 0, 0, at(i))),
            pl.BlockSpec((views, block), lambda i: (0, at(i))),
        ],
        out_specs=(
            pl.BlockSpec((row_block, params), lambda i: (0, 0)),
            pl.BlockSpec((total,), lambda i: (0,)),
        ),
        scratch_shapes=[pltpu.VMEM((d, params), jnp.float32) for d in depths]
        + [pltpu.VMEM((params, 2 * block), jnp.bfloat16) for d in depths]
        + [pltpu.VMEM((d, 2 * block), jnp.bfloat16) for d in depths]
        + [pltpu.VMEM(s, jnp.float32) for s in shapes]
        + [pltpu.VMEM((IMAGES,) + s, t) for s, t in zip(shapes, types)]
        + [pltpu.VMEM(s[1:], jnp.float32) for s in shapes]
        + [pltpu.VMEM(s[1:], t) for s, t in zip(shapes, types)]
        + [pltpu.VMEM((regions - 1,) + s[2:], t) for s, t in zip(shapes, types)]
        + [
            pltpu.VMEM((total + EXTRA, total), jnp.float32),
            pltpu.VMEM((total + EXTRA, params), jnp.bfloat16),
            pltpu.VMEM((total + EXTRA, params), jnp.bfloat16),
            pltpu.VMEM((params, params), jnp.bfloat16),
            pltpu.VMEM((params, params), jnp.bfloat16),
            pltpu.VMEM((TILE, TILE), jnp.float32),
            pltpu.VMEM((TILE, TILE), jnp.float32),
            dma((count,)),
            dma((count,)),
            dma((count, CHUNKS)),
            dma((count, regions - 1)),
            dma((count, regions - 1)),
            dma((count, CHUNKS)),
            dma((count, IMAGES - 1)),
            dma((count, IMAGES)),
            dma((count, IMAGES)),
            dma((count, IMAGES)),
            dma((peers,)),
            dma((IMAGES, CHUNKS)),
        ],
        compiler_params=pltpu.CompilerParams(
            collective_id=0,
            has_side_effects=True,
            vmem_limit_bytes=VMEM_LIMIT,
            dimension_semantics=("arbitrary",),
        ),
        name="reduce_and_factor",
    )(track_counts, cam_jac, point_rows, track_images)


def emit_kernel(held_ref, whole_ref, factor_ref, solved_ref):
    factor_ref[...] = held_ref[...]
    solved_ref[...] = whole_ref[...]


def emit(held, whole):
    vmem = pl.BlockSpec(memory_space=pltpu.VMEM)
    return pl.pallas_call(
        emit_kernel,
        out_shape=(
            jax.ShapeDtypeStruct(held.shape, held.dtype),
            jax.ShapeDtypeStruct(whole.shape, whole.dtype),
        ),
        in_specs=[vmem, vmem],
        out_specs=(vmem, vmem),
        name="emit",
    )(held, whole)


def on_device(cam_jac, point_rows, track_images, track_counts):
    regions = lax.axis_size("region")
    params = cam_jac.shape[2]
    row_block = IMAGES * params // (regions * lax.axis_size("row"))
    factor, solved = emit(
        *run_steps(cam_jac, point_rows, track_images, track_counts, regions, row_block)
    )
    return (factor, solved)


def solution(mesh):
    in_specs = (
        P(None, None, None, "region"),
        P(None, None, None, "region"),
        P(None, "region"),
        P(),
    )
    out_specs = (P(("region", "row"), "col"), P())
    return jax.shard_map(
        on_device, mesh=mesh, in_specs=in_specs, out_specs=out_specs, check_vma=False
    )
```

```python
import functools

import jax
import jax.numpy as jnp
from jax import lax
from jax.experimental import pallas as pl
from jax.experimental.pallas import tpu as pltpu
from jax.sharding import PartitionSpec as P

IMAGES = 4
CHUNKS = 4
ROWS = 8
BLOCK = 512
TILE = 128
EXTRA = 16
VMEM_LIMIT = 60 * 1024 * 1024

damping = 0.1
point_damping = 0.5

NT = (((1,), (1,)), ((), ()))
NN = (((1,), (0,)), ((), ()))
MESH = pl.DeviceIdType.MESH


def point_terms(pts):
    views = len(pts)
    pairs = [(k, r) for k in range(views) for r in range(2)]

    def entry(left, right):
        return sum(pts[k][r][left] * pts[k][r][right] for k, r in pairs)

    d1 = jnp.sqrt(entry(0, 0) + point_damping)
    b1 = entry(1, 0) / d1
    bf = entry(2, 0) / d1
    d2 = jnp.sqrt(entry(1, 1) + point_damping - b1 * b1)
    b2 = (entry(2, 1) - bf * b1) / d2
    d3 = jnp.sqrt(entry(2, 2) + point_damping - bf * bf - b2 * b2)

    def solve(first, second, third):
        o1 = first / d1
        o2 = (second - b1 * o1) / d2
        o3 = (third - bf * o1 - b2 * o2) / d3
        return [o.astype(jnp.bfloat16).astype(jnp.float32) for o in (o1, o2, o3)]

    coef = {(k, r): solve(*pts[k][r][0:3]) for k, r in pairs}
    step = solve(*[entry(c, 3) for c in range(3)])
    return coef, step


def part_at(u):
    return u // 2, u % 2 == 0


def part_shapes(params):
    shapes = []
    for u in range(2 * IMAGES - 1):
        b, diagonal = part_at(u)
        tail = (ROWS, params) if diagonal else ((IMAGES - 1 - b) * 2 * ROWS, params // 2)
        shapes.append((2, CHUNKS) + tail)
    return shapes


def accumulate_block(block, turn, images_at, pos_ref, cam_ref, pts_ref, img_ref, accs, rhs, lhs):
    params=cam_ref.shape[2]
    views=cam_ref.shape[0]
    own=params//4
    count=pos_ref[lax.axis_index("region")]
    row_at=lax.axis_index("row"); col_at=lax.axis_index("col")
    start=(2*turn+row_at)*block
    sub=16
    slot=start+lax.broadcasted_iota(jnp.int32,(1,block),1)
    live=slot<count
    pts=[]
    for k in range(views):
        pts.append([])
        for r in range(2):
            wide=pts_ref[k,r].astype(jnp.float32)
            pts[k].append([wide[c:c+1,:] for c in range(4)])
    coef,y=point_terms(pts)
    images=[img_ref[k:k+1,:] for k in range(views)]
    zero=jnp.zeros((sub-2,block),jnp.float32)
    def pick(masks,values):
        out=jnp.zeros_like(values[0])
        for mask,value in zip(masks,values): out=jnp.where(mask,value,out)
        return out
    def widen(mask):
        return jnp.broadcast_to(mask.astype(jnp.float32),(sub,block)).astype(jnp.bfloat16)>0
    masks=[[(images[k]==a)&live for k in range(views)] for a in range(IMAGES)]
    wide=[[widen(m) for m in masks[a][:2]] for a in range(IMAGES)]
    c=[[[pick(masks[a],[coef[k,r][m] for k in range(views)]) for m in range(3)] for r in range(2)] for a in range(IMAGES)]
    held=[(masks[a][0]|masks[a][1]|masks[a][2]).astype(jnp.float32) for a in range(IMAGES)]
    err=[[pick(masks[a],[pts[k][r][3] for k in range(views)]) for r in range(2)] for a in range(IMAGES)]
    def chosen(a,at,r):
        j=[cam_ref[k,r,pl.ds(at,sub),:] for k in range(views)]
        return jnp.where(wide[a][0],j[0],jnp.where(wide[a][1],j[1],j[2]))
    mine=pl.multiple_of(col_at*own,own)
    for b in images_at:
        for i in range(params//sub):
            for r in range(2):
                rhs[b][i*sub:(i+1)*sub,r*block:(r+1)*block]=chosen(b,i*sub,r)
        for a in range(b,IMAGES):
            x={}
            for r in range(2):
                for s in range(2):
                    if a==b and s<r: x[r,s]=x[s,r]; continue
                    v=-(c[a][r][0]*c[b][s][0]+c[a][r][1]*c[b][s][1]+c[a][r][2]*c[b][s][2])
                    x[r,s]=v+held[a] if a==b and r==s else v
            for i in range(own//sub):
                jac=[chosen(a,mine+i*sub,r).astype(jnp.float32) for r in range(2)]
                for s in range(2):
                    v=jac[0]*x[0,s]+jac[1]*x[1,s]
                    lhs[b][(a-b)*own+i*sub:(a-b)*own+(i+1)*sub,s*block:(s+1)*block]=v.astype(jnp.bfloat16)
        depth=(IMAGES-b)*own
        for r in range(2):
            g=err[b][r]-(c[b][r][0]*y[0]+c[b][r][1]*y[1]+c[b][r][2]*y[2])
            near=g.astype(jnp.bfloat16).astype(jnp.float32)
            lhs[b][depth:depth+sub,r*block:(r+1)*block]=jnp.concatenate([near,g-near,zero],axis=0).astype(jnp.bfloat16)
        accs[b][...]+=lax.dot_general(lhs[b][...],rhs[b][...],NT,preferred_element_type=jnp.float32)


def split_parts(params, images_at, accs, outs):
    own = params // 4
    col_at = lax.axis_index("col")
    half=params//2
    for b in images_at:
        acc=accs[b]
        depth=(IMAGES-b)*own
        sub8=lax.broadcasted_iota(jnp.int32,(8,half),0)
        grad=acc[depth:depth+1,:]+acc[depth+1:depth+2,:]
        one=jnp.broadcast_to(grad[:,0:half],(8,half))
        two=jnp.broadcast_to(grad[:,half:params],(8,half))
        held=acc[0:8,half:params]
        grad=jnp.where(sub8==0,one,jnp.where(sub8==1,two,held))
        acc[0:8,half:params]=jnp.where(col_at==0,grad,held)
    for u, out in enumerate(outs):
        b, diagonal = part_at(u)
        if b not in images_at:
            continue
        acc = accs[b]
        for core in range(2):
            for q in range(CHUNKS):
                if diagonal:
                    src = (core * CHUNKS + q) * ROWS
                    out[core, q] = acc[src : src + ROWS, :]
                else:
                    wide = 2 * ROWS
                    at = q % 2 * half
                    for i in range(IMAGES - 1 - b):
                        src = (i + 1) * own + (core * 2 + q // 2) * wide
                        out[core, q, i * wide : (i + 1) * wide, :] = acc[src : src + wide, at : at + half]


def split(x):
    high = x.astype(jnp.bfloat16)
    return high, (x - high.astype(jnp.float32)).astype(jnp.bfloat16)


def product(left, right, dims):
    lh, ll = left
    rh, rl = right
    (lc, rc), _ = dims
    return lax.dot_general(
        jnp.concatenate([lh, ll, lh], axis=lc[0]),
        jnp.concatenate([rh, rh, rl], axis=rc[0]),
        dims,
        preferred_element_type=jnp.float32,
    )


def product_parts(left, right, dims):
    lh, ll = left
    rh, rl = right
    dot = functools.partial(lax.dot_general, dimension_numbers=dims, preferred_element_type=jnp.float32)
    return dot(lh, rh) + (dot(ll, rh) + dot(lh, rl))


def eliminate(tile):
    near = 2
    W=(8,TILE)
    sub=lax.broadcasted_iota(jnp.int32,W,0); lane=lax.broadcasted_iota(jnp.int32,W,1)
    other=sub+1-2*lax.rem(sub,2)
    zero=jnp.zeros(W,jnp.float32)
    V=TILE//8
    f=[tile[8*i:8*i+8,:] for i in range(V)]
    def swap(x): return jnp.take_along_axis(x,other,axis=0,mode="promise_in_bounds")
    def down(x,p): return jnp.broadcast_to(x[p:p+1,:],W)
    def along(x,l): return jnp.broadcast_to(x[:,l:l+1],W)
    def pivots(c,rest,R,RB):
        main=cross=lower=scale=zero
        for p in range(0,8,2):
            cp,cq=c[p],c[p+1]
            a,b,d=down(cp,p),down(cp,p+1),down(cq,p+1)
            det=a*d-b*b
            inv=1.0/det
            rp,rq=down(R,p),down(R,p+1)
            if p<6:
                keep=sub>p+1
                u=jnp.where(keep,d*cp-b*cq,0.0); v=jnp.where(keep,a*cq-b*cp,0.0)
                ui,vi=u*inv,v*inv
                for s in range(p+2,8):
                    cs,ct=down(cp,s),down(cq,s)
                    c[s]=c[s]-(u*cs+v*ct)*inv if s<p+4 else c[s]-ui*cs-vi*ct
                R=R-ui*rp-vi*rq
            if rest is not None:
                n,m=rest
                un,vn=d*n[p]-b*n[p+1],a*n[p+1]-b*n[p]
                uni,vni=un*inv,vn*inv
                for s in range(p+2,8): n[s]=n[s]-uni*down(cp,s)-vni*down(cq,s)
                for s in range(8):
                    ns,nt=down(n[p],s),down(n[p+1],s)
                    if p==6 and s<2: m[s]=m[s]-(un*ns+vn*nt)*inv
                    else: m[s]=m[s]-uni*ns-vni*nt
                RB=RB-uni*rp-vni*rq
            ia=1.0/a
            m0,m1=sub==p,sub==p+1
            main=jnp.where(m0,d*inv,jnp.where(m1,a*inv,main))
            cross=jnp.where(m0|m1,b*inv,cross)
            lower=jnp.where(m1,b*ia,lower)
            scale=jnp.where(m0,ia,jnp.where(m1,a*inv,scale))
        def pairs(x): return main*x-cross*swap(x)
        w=pairs(R)
        for q in (6,4,2):
            l0=jnp.where(sub<q,pairs(c[q]),0.0); l1=jnp.where(sub<q,pairs(c[q+1]),0.0)
            w=w-l0*down(w,q)-l1*down(w,q+1)
        out=(R-lower*swap(R))*jnp.sqrt(scale)
        return w,out,RB
    for g in range(V//2):
        j=16*g
        top,bot=f[2*g],f[2*g+1]
        in0=(lane>=j)&(lane<j+8); in1=(lane>=j+8)&(lane<j+16); both=in0|in1
        c=[along(top,j+s) for s in range(8)]
        n=[along(bot,j+s) for s in range(8)]
        m=[along(bot,j+8+s) for s in range(8)]
        R0=jnp.where(in0,(lane-j==sub).astype(jnp.float32),top)
        RB=jnp.where(in0,0.0,bot)
        w0,out0,RB=pivots(c,(n,m),R0,RB)
        R1=jnp.where(in1,(lane-j-8==sub).astype(jnp.float32),RB)
        lift=[along(w0,j+8+q) for q in range(8)]
        w1,out1,_=pivots(m,None,R1,None)
        w0=jnp.where(in1,0.0,w0)
        for q in reversed(range(8)): w0=w0-lift[q]*down(w1,q)
        w=[w0,w1]
        last=min(V,2*g+2+near)
        if last<V:
            wide=[zero]*V
            wide[2*g],wide[2*g+1]=w
            up=product_parts(split(jnp.concatenate(f[last:],axis=0)),split(jnp.concatenate(wide,axis=0)),NN)
        spread=[down(w[p//8],p%8) for p in range(16)]
        for i in range(2*g+2,last):
            value=jnp.where(both,0.0,f[i])
            for p in reversed(range(16)): value=value-along(f[i],j+p)*spread[p]
            f[i]=value
        for i in range(last,V): f[i]=jnp.where(both,0.0,f[i])-up[8*(i-last):8*(i-last)+8]
        f[2*g],f[2*g+1]=out0,out1
    return jnp.concatenate([jnp.where(lane<=sub+8*i,f[i],0.0) for i in range(V)],axis=0)


def finish_kernel(regions, params, turns, work, divide, *refs):
    shapes = part_shapes(params)
    count = len(shapes)
    parts, refs = refs[:count], refs[count:]
    factor_ref, solved_ref = refs[:2]
    refs = refs[2:]
    alls, refs = refs[:count], refs[count:]
    recv1, refs = refs[:count], refs[count:]
    mine, refs = refs[:count], refs[count:]
    recv2, refs = refs[:count], refs[count:]
    a_ref, high_ref, low_ref, inv_high, inv_low, tile_ref, link_ref = refs[:7]
    s1, r1, s2, r2, s3, r3, s4, r4, s5, r5, s6, r6 = refs[7:]
    total = IMAGES * params
    own = params // 4
    half = params // 2
    stride = regions // CHUNKS
    region_at = lax.axis_index("region")
    row_at = lax.axis_index("row")
    col_at = lax.axis_index("col")
    chunk_at = region_at // stride
    owner = lax.rem(region_at, stride) == 0
    other = lax.rem(region_at, stride) != 0

    def device(region, row, col):
        return {"region": region, "row": row, "col": col}

    def remote(src, dst, send, recv, to):
        return pltpu.make_async_remote_copy(
            src_ref=src, dst_ref=dst, send_sem=send, recv_sem=recv, device_id=to, device_id_type=MESH
        )

    def landed(ref, recv):
        remote(ref, ref, s1.at[0], recv, partner).wait_recv()

    def guarded(when, action):
        if when is True:
            action()
        else:
            pl.when(when)(action)

    owns = True if stride == 1 else owner
    partner = device(region_at, 1 - row_at, col_at)
    along = [device(lax.rem(region_at + d, regions), row_at, col_at) for d in range(1, regions)]
    cols = [lax.rem(col_at + d, IMAGES) for d in range(IMAGES)]
    across = [device(region_at, row_at, c) for c in cols[1:]]
    others = [
        device(lax.rem(region_at + d, regions), row_at, cols[e])
        for d in range(regions)
        for e in range(IMAGES)
        if d + e > 0
    ]
    sent = []

    def send(when, src, dst, sems, index, recv, to, like):
        sent.append((when, like, sems, index))
        guarded(when, lambda: remote(src, dst, sems.at[index], recv, to).start())

    def swap_cores(u):
        send(True, parts[u].at[1 - row_at], recv1[u], s1, (u,), r1.at[u], partner, lambda: recv1[u])

    def reduce_cores(u):
        landed(recv1[u], r1.at[u])
        mine[u][...] = (parts[u][row_at] + recv1[u][...]).astype(mine[u].dtype)
        for d in range(0 if stride > 1 else 1, CHUNKS):
            chunk = lax.rem(chunk_at + d, CHUNKS)
            to = chunk * stride
            gap = lax.rem(to - region_at + regions, regions)
            send(
                True if d else other,
                mine[u].at[chunk],
                recv2[u].at[gap - 1],
                s2,
                (u, d),
                r2.at[u, gap - 1],
                device(to, row_at, col_at),
                lambda: mine[u].at[0],
            )

    def reduce_regions(u):
        def add():
            value = mine[u][chunk_at].astype(jnp.float32)
            for gap in range(regions - 1):
                landed(recv2[u].at[gap], r2.at[u, gap])
                value = value + recv2[u][gap].astype(jnp.float32)
            alls[u][col_at, row_at, chunk_at] = value.astype(alls[u].dtype)

        guarded(owns, add)
        piece = alls[u].at[col_at, row_at, chunk_at]
        if u == 0:
            for i, peer in enumerate(others):
                send(owns, piece, piece, s6, (i,), r6.at[col_at, chunk_at], peer, lambda: mine[u].at[0])
        else:
            for d, peer in enumerate(along):
                send(owns, piece, piece, s3, (u, d,), r3.at[u, chunk_at], peer, lambda: mine[u].at[0])

    def forward(u, d):
        piece = alls[u].at[cols[d], row_at]
        send(True, piece, piece, s5, (u, d,), r5.at[u, cols[d]], partner, lambda: mine[u])

    def gather_regions(u):
        def arrive(e, d):
            chunk = lax.rem(chunk_at + d, CHUNKS)
            landed(alls[u].at[cols[e], row_at, chunk], r6.at[cols[e], chunk] if u == 0 else r3.at[u, chunk])

        for e in range(IMAGES if u == 0 else 1):
            for d in range(CHUNKS):
                if d + e > 0:
                    arrive(e, d)
                elif stride > 1:
                    guarded(other, lambda: arrive(0, 0))
            forward(u, e)
        if u > 0:
            piece = alls[u].at[col_at, row_at]
            for d, peer in enumerate(across):
                send(True, piece, piece, s4, (u, d,), r4.at[u, col_at], peer, lambda: mine[u])

    def gather_cols(u):
        for d in range(1, IMAGES):
            landed(alls[u].at[cols[d], row_at], r4.at[u, cols[d]])
            forward(u, d)

    def place(u):
        for d in range(IMAGES):
            landed(alls[u].at[cols[d], 1 - row_at], r5.at[u, cols[d]])
        b, diagonal = part_at(u)
        left = b * params
        for col in range(IMAGES):
            for core in range(2):
                for q in range(CHUNKS):
                    value = alls[u][col, core, q].astype(jnp.float32)
                    if diagonal:
                        row = b * params + col * own + (core * CHUNKS + q) * ROWS
                        a_ref[row : row + ROWS, left : left + params] += value
                    else:
                        wide = 2 * ROWS
                        at = left + q % 2 * half
                        for i in range(IMAGES - 1 - b):
                            row = (b + 1 + i) * params + col * own + (core * 2 + q // 2) * wide
                            a_ref[row : row + wide, at : at + half] += value[i * wide : (i + 1) * wide]
        if diagonal:
            for t in range(2):
                at = left + t * half
                a_ref[total : total + 1, at : at + half] += alls[u][0, 0, 0, t : t + 1, half:params]

    step = pl.program_id(0)
    last = turns - 1
    phases = [[0, 1], [2, 3]]
    marks = {
        last: [(swap_cores, u) for u in range(4)],
        turns: [(reduce_cores, 0), (reduce_cores, 1)],
        turns + 1: [(reduce_cores, 2), (reduce_cores, 3)],
        turns + last: [(reduce_regions, 0), (reduce_regions, 1), (swap_cores, 4), (swap_cores, 5), (swap_cores, 6)],
    }
    for phase, images_at in enumerate(phases):

        @pl.when(step // turns == phase)
        def _():
            work(lax.rem(step, turns), images_at)

        for turn in range(turns):
            mark = phase * turns + turn
            if turn < last and mark not in marks:
                continue

            @pl.when(step == mark)
            def _():
                if turn == last:
                    divide(images_at)
                if mark == last:
                    pl.semaphore_wait(pltpu.get_barrier_semaphore(), 1 + len(others))
                for action, u in marks[mark]:
                    action(u)

    def flush(chosen):
        kept = []
        for when, like, sems, index in sent:
            if chosen(sems, index):
                guarded(when, lambda: remote(like(), like(), sems.at[index], r1.at[0], partner).wait_send())
            else:
                kept.append((when, like, sems, index))
        sent[:] = kept

    def finish():
        for u in range(4, count):
            reduce_cores(u)
        reduce_regions(2)
        reduce_regions(3)
        flush(lambda sems, index: sems is s1 or sems is s2 and index[0] < 4)
        gather_regions(0)
        flush(lambda sems, index: sems is s6 or sems is s2)
        gather_regions(1)
        place(0)
        middle = {
            0: [(gather_regions, 2), (gather_regions, 3), (reduce_regions, 4), (reduce_regions, 5), (reduce_regions, 6)],
            1: [],
            2: [],
        }
        before = {
            0: [(gather_cols, 1), (place, 1), (gather_cols, 2)],
            1: [(gather_cols, 4), (gather_cols, 5), (place, 3)],
            2: [(place, 5)],
        }
        after = {
            0: [(gather_cols, 3), (gather_regions, 4), (gather_regions, 5), (gather_regions, 6), (place, 2)],
            1: [(gather_cols, 6), (place, 4)],
            2: [(place, 6)],
        }
        eye_r = lax.broadcasted_iota(jnp.int32, (TILE, TILE), 0)
        eye_c = lax.broadcasted_iota(jnp.int32, (TILE, TILE), 1)
        damp = jnp.where(eye_r == eye_c, damping, 0.0).astype(jnp.float32)

        def panel(n, _):
            def at(t):
                return pl.ds(pl.multiple_of(n * params + t * TILE, TILE), TILE)

            def keep(t, e, value):
                high, low = split(value)
                inv_high[t * TILE : (t + 1) * TILE, e * TILE : (e + 1) * TILE] = high
                inv_low[t * TILE : (t + 1) * TILE, e * TILE : (e + 1) * TILE] = low

            first = a_ref[at(0), at(0)] + damp
            a_ref[at(0), at(0)] = first
            inv0 = eliminate(first)
            keep(0, 0, inv0)
            keep(0, 1, jnp.zeros((TILE, TILE), jnp.float32))
            split0 = split(inv0)
            below = split(product(split(a_ref[at(1), at(0)]), split0, NT))
            second = a_ref[at(1), at(1)] + damp
            a_ref[at(1), at(1)] = second
            tile_ref[...] = second - product(below, below, NT)
            link_ref[...] = product(below, split0, NN)
            for s in middle:

                @pl.when(n == s)
                def _():
                    for action, u in middle[s]:
                        action(u)

            inv1 = eliminate(tile_ref[...])
            keep(1, 1, inv1)
            keep(1, 0, -product(split(inv1), split(link_ref[...]), NN))
            for s in range(IMAGES):

                @pl.when(n == s)
                def _():
                    for action, u in before.get(s, []):
                        action(u)
                    lo = s * params
                    hi = lo + params
                    end = total + EXTRA
                    value = product(split(a_ref[lo:end, lo:hi]), (inv_high[...], inv_low[...]), NT)
                    a_ref[lo:end, lo:hi] = value
                    high, low = split(value)
                    high_ref[lo:end, :] = high
                    low_ref[lo:end, :] = low
                    for c in range(s + 1, IMAGES):
                        col = slice(c * params, (c + 1) * params)
                        row = slice(c * params, end)
                        a_ref[row, col] -= product(
                            (high_ref[row, :], low_ref[row, :]), (high_ref[col, :], low_ref[col, :]), NT
                        )
                    for action, u in after.get(s, []):
                        action(u)

            return 0

        lax.fori_loop(0, IMAGES, panel, 0)
        flush(lambda sems, index: True)
        row_block = factor_ref.shape[0]
        first_row = pl.multiple_of((region_at * 2 + row_at) * row_block, row_block)
        first_col = pl.multiple_of(col_at * params, params)
        held = a_ref[pl.ds(first_row, row_block), pl.ds(first_col, params)]
        at_row = first_row + lax.broadcasted_iota(jnp.int32, held.shape, 0)
        at_col = first_col + lax.broadcasted_iota(jnp.int32, held.shape, 1)
        factor_ref[...] = jnp.where(at_row >= at_col, held, 0.0)
        solved_ref[...] = a_ref[total, :]

    pl.when(step == pl.num_programs(0) - 1)(finish)


def greet(regions):
    region_at = lax.axis_index("region")
    row_at = lax.axis_index("row")
    col_at = lax.axis_index("col")
    barrier = pltpu.get_barrier_semaphore()
    pl.semaphore_signal(
        barrier,
        inc=1,
        device_id={"region": region_at, "row": 1 - row_at, "col": col_at},
        device_id_type=MESH,
    )
    for d in range(regions):
        for e in range(IMAGES):
            if d + e > 0:
                peer = {
                    "region": lax.rem(region_at + d, regions),
                    "row": row_at,
                    "col": lax.rem(col_at + e, IMAGES),
                }
                pl.semaphore_signal(barrier, inc=1, device_id=peer, device_id_type=MESH)


def step_kernel(regions, block, turns, pos_ref, cam_ref, pts_ref, img_ref, factor_ref, solved_ref, *refs):
    params = cam_ref.shape[2]
    count = 2 * IMAGES - 1
    accs, rhs, lhs = refs[:IMAGES], refs[IMAGES : 2 * IMAGES], refs[2 * IMAGES : 3 * IMAGES]
    parts, refs = refs[3 * IMAGES : 3 * IMAGES + count], refs[3 * IMAGES + count :]

    @pl.when(pl.program_id(0) == 0)
    def _():
        greet(regions)
        refs[4 * count][...] = jnp.zeros_like(refs[4 * count])
        for acc in accs:
            acc[...] = jnp.zeros_like(acc)

    def work(turn, images_at):
        accumulate_block(block, turn, images_at, pos_ref, cam_ref, pts_ref, img_ref, accs, rhs, lhs)

    def divide(images_at):
        split_parts(params, images_at, accs, parts)

    finish_kernel(regions, params, turns, work, divide, *parts, factor_ref, solved_ref, *refs)


def run_steps(cam_jac, point_rows, track_images, track_counts, regions, row_block):
    views, _, params, slots = cam_jac.shape
    block = min(BLOCK, slots // 2)
    turns = slots // block // 2
    own = params // 4
    shapes = part_shapes(params)
    count = len(shapes)
    types = [jnp.float32 if part_at(u)[1] else jnp.bfloat16 for u in range(count)]
    total = IMAGES * params
    dma = pltpu.SemaphoreType.DMA
    peers = regions * IMAGES - 1
    depths = [(IMAGES - b) * own + 16 for b in range(IMAGES)]

    def at(i):
        return 2 * lax.rem(i, turns) + lax.axis_index("row")

    return pl.pallas_call(
        functools.partial(step_kernel, regions, block, turns),
        out_shape=(
            jax.ShapeDtypeStruct((row_block, params), jnp.float32),
            jax.ShapeDtypeStruct((total,), jnp.float32),
        ),
        grid=(2 * turns,),
        in_specs=[
            pl.BlockSpec(memory_space=pltpu.SMEM),
            pl.BlockSpec((views, 2, params, block), lambda i: (0, 0, 0, at(i))),
            pl.BlockSpec((views, 2, 4, block), lambda i: (0, 0, 0, at(i))),
            pl.BlockSpec((views, block), lambda i: (0, at(i))),
        ],
        out_specs=(
            pl.BlockSpec((row_block, params), lambda i: (0, 0)),
            pl.BlockSpec((total,), lambda i: (0,)),
        ),
        scratch_shapes=[pltpu.VMEM((d, params), jnp.float32) for d in depths]
        + [pltpu.VMEM((params, 2 * block), jnp.bfloat16) for d in depths]
        + [pltpu.VMEM((d, 2 * block), jnp.bfloat16) for d in depths]
        + [pltpu.VMEM(s, jnp.float32) for s in shapes]
        + [pltpu.VMEM((IMAGES,) + s, t) for s, t in zip(shapes, types)]
        + [pltpu.VMEM(s[1:], jnp.float32) for s in shapes]
        + [pltpu.VMEM(s[1:], t) for s, t in zip(shapes, types)]
        + [pltpu.VMEM((regions - 1,) + s[2:], t) for s, t in zip(shapes, types)]
        + [
            pltpu.VMEM((total + EXTRA, total), jnp.float32),
            pltpu.VMEM((total + EXTRA, params), jnp.bfloat16),
            pltpu.VMEM((total + EXTRA, params), jnp.bfloat16),
            pltpu.VMEM((params, params), jnp.bfloat16),
            pltpu.VMEM((params, params), jnp.bfloat16),
            pltpu.VMEM((TILE, TILE), jnp.float32),
            pltpu.VMEM((TILE, TILE), jnp.float32),
            dma((count,)),
            dma((count,)),
            dma((count, CHUNKS)),
            dma((count, regions - 1)),
            dma((count, regions - 1)),
            dma((count, CHUNKS)),
            dma((count, IMAGES - 1)),
            dma((count, IMAGES)),
            dma((count, IMAGES)),
            dma((count, IMAGES)),
            dma((peers,)),
            dma((IMAGES, CHUNKS)),
        ],
        compiler_params=pltpu.CompilerParams(
            collective_id=0,
            has_side_effects=True,
            vmem_limit_bytes=VMEM_LIMIT,
            dimension_semantics=("arbitrary",),
        ),
        name="reduce_and_factor",
    )(track_counts, cam_jac, point_rows, track_images)


def emit_kernel(held_ref, whole_ref, factor_ref, solved_ref):
    factor_ref[...] = held_ref[...]
    solved_ref[...] = whole_ref[...]


def emit(held, whole):
    vmem = pl.BlockSpec(memory_space=pltpu.VMEM)
    return pl.pallas_call(
        emit_kernel,
        out_shape=(
            jax.ShapeDtypeStruct(held.shape, held.dtype),
            jax.ShapeDtypeStruct(whole.shape, whole.dtype),
        ),
        in_specs=[vmem, vmem],
        out_specs=(vmem, vmem),
        name="emit",
    )(held, whole)


def on_device(cam_jac, point_rows, track_images, track_counts):
    regions = lax.axis_size("region")
    params = cam_jac.shape[2]
    row_block = IMAGES * params // (regions * lax.axis_size("row"))
    factor, solved = emit(
        *run_steps(cam_jac, point_rows, track_images, track_counts, regions, row_block)
    )
    return (factor, solved)


def solution(mesh):
    in_specs = (
        P(None, None, None, "region"),
        P(None, None, None, "region"),
        P(None, "region"),
        P(),
    )
    out_specs = (P(("region", "row"), "col"), P())
    return jax.shard_map(
        on_device, mesh=mesh, in_specs=in_specs, out_specs=out_specs, check_vma=False
    )
```
